128 devices in a mesh: row: 8 (over y, core), col: 16 (over x, z).
Axes of the slice: x: 4, y: 4, z: 4, core: 2. Of those that a mesh axis runs over, the one named last changes fastest.
Arguments:
- rhs: float32 [512, 8192], P('col', 'row'), may hold values from -6 to 6
- couple_prev: float32 [8192, 1024], P('row'), may hold values from -0.1875 to 0.1875
- diag_inverse: float32 [8192, 1024], P('row'), may hold values from -2 to 2
- coupling: bfloat16 [1536, 16, 128], P(('row', 'col')), may hold values from -0.5 to 0.5
- pair_block: int32 [1536], P(('row', 'col')), may hold values from 0 to 63, as said below
- pair_tile: int32 [1536], P(('row', 'col')), may hold values from 0 to 2
- pair_count: int32 [128], P(('row', 'col')), may hold values from 8 to 12, as said below
- owner_slot: int32 [8, 48], P('row'), may hold values from 0 to 47, each once within a row
- schur: bfloat16 [6144, 65536], P('row', 'col'), may hold values from -6 to 6
- surface_factor: bfloat16 [512, 65536], P(None, 'col'), may hold values from -0.125 to 0.125
Outputs:
- updated: bfloat16 [6144, 65536], P('row', 'col')
The draws below stay inside these ranges and needn't reach their ends.
Inputs may be any that keep to these rules, and one draw needn't show every extreme that they name: Among the first pair_count entries of one owner, at most 3 name blocks whose block-row group pair_block // 8 is the same; some owner has exactly 3 from one group. `pair_count`: some owner has 12 live coupling tiles.
All inputs are finite; a program needn't handle non-finite values.
Results may differ from the reference program's by a relative error of at most 0.0055.
Values may be sent and summed in bfloat16 or wider, within the bound.
No kernel may reach another device: no remote copies, remote signals or barrier semaphores. Data moves between devices by JAX's collectives and lax.ppermute only.
A program may use at most 128 MiB of HBM per device.

```python
import jax
import jax.numpy as jnp
from jax import lax

NB = 1024
BLK = 128
NRHS = 512
TILE = 16
TPD = 3
KCAP = 12
CAP = 3
NS = 8192
NSURF = 65536
TPR = 48
SR = 768
N_ROW = 8
N_COL = 16


def pair_lists(key):
    owners = N_ROW * N_COL
    base = jax.random.fold_in(key, 4099)
    keys = jax.random.split(base, 6)
    least = 2 * KCAP // 3
    count = jax.random.randint(keys[0], (owners,), least, KCAP + 1)
    full = jax.random.randint(keys[1], (owners,), 0, 8) == 0
    forced = jax.random.randint(keys[2], (), 0, owners)
    full = full | (jnp.arange(owners) == forced)
    count = jnp.where(full, KCAP, count)
    lowest = (forced + 1) % owners
    count = jnp.where(jnp.arange(owners) == lowest, least, count).astype(jnp.int32)
    row_keys = jax.random.split(keys[3], owners)
    others = jax.vmap(lambda k: jax.random.permutation(k, N_ROW - 1))(row_keys) + 1
    offsets = jnp.concatenate([jnp.zeros((owners, 1), jnp.int32), others.astype(jnp.int32)], axis=1)
    group = jnp.arange(KCAP) // CAP
    owner_row = jnp.arange(owners) // N_COL
    source = (owner_row[:, None] + offsets[:, group]) % N_ROW
    order_keys = jax.random.split(keys[4], owners)
    order = jax.vmap(lambda k: jax.random.permutation(k, KCAP))(order_keys)
    source = jnp.take_along_axis(source, order, axis=1)
    local = jax.random.randint(keys[5], (owners, KCAP), 0, NB // BLK)
    blocks = (source * (NB // BLK) + local).astype(jnp.int32)
    tiles = jax.random.randint(jax.random.fold_in(keys[5], 1), (owners, KCAP), 0, TPD).astype(jnp.int32)
    return (blocks.reshape(-1), tiles.reshape(-1), count)


def draw_pair_block(key, part):
    return pair_lists(key)[0]


def draw_pair_tile(key, part):
    return pair_lists(key)[1]


def draw_pair_count(key, part):
    return pair_lists(key)[2]


def draw_diag_inverse(key, part):
    total = NB * N_ROW
    first, second = jax.random.split(jax.random.fold_in(key, 11))
    spread = jax.random.normal(first, (total, NB), jnp.float32) * (0.3 / NB ** 0.5)
    middle = jax.random.uniform(second, (total,), jnp.float32, 0.75, 1.25)
    eye = (jnp.arange(total)[:, None] % NB == jnp.arange(NB)[None, :]).astype(jnp.float32)
    return spread + eye * middle[:, None]


def block_scale(rng, shape, cuts, low, largest):
    def one(axis_at, parts):
        steps = jax.random.uniform(jax.random.fold_in(jax.random.fold_in(rng, 6), axis_at), (parts,), jnp.float32, low / len(cuts), largest / len(cuts))
        return jnp.repeat(jnp.exp(steps), shape[axis_at] // parts).reshape((-1,) + (1,) * (len(shape) - axis_at - 1))

    gain = one(*cuts[0])
    for cut in cuts[1:]:
        gain = gain * one(*cut)
    return gain


def centred(rng, shape, deviation, limit, cuts=(), kind=jnp.bfloat16):
    loudness = block_scale(rng, shape, cuts, -0.22, 0.18) if cuts else 1.0
    values = jax.random.normal(rng, shape, jnp.float32) * deviation * loudness
    return jnp.minimum(jnp.maximum(values, -limit), limit).astype(kind)


def setup_inputs(seed: int = 0) -> dict:
    key_of = jax.random.split(jax.random.key(seed), 11)
    rhs = centred(key_of[0], (NRHS, NS), 1.0, 6.0, ((0, 16), (1, 8)), jnp.float32)
    couple_prev = centred(key_of[1], (NS, NB), NB ** -0.5, 0.1875, ((0, 8),), jnp.float32)
    diag_inverse = draw_diag_inverse(jax.random.fold_in(key_of[10], 71), 0)
    coupling = centred(key_of[3], (N_ROW * N_COL * KCAP, TILE, BLK), BLK ** -0.5, 0.5, ((0, 128),))
    pair_block = draw_pair_block(jax.random.fold_in(key_of[10], 71), 0)
    pair_tile = draw_pair_tile(jax.random.fold_in(key_of[10], 71), 0)
    pair_count = draw_pair_count(jax.random.fold_in(key_of[10], 71), 0)
    owner_slot = jax.vmap(lambda own: jax.random.permutation(own, TPR))(jax.random.split(key_of[7], N_ROW)).reshape((N_ROW, TPR)).astype(jnp.int32)
    schur = centred(key_of[8], (N_ROW * SR, NSURF), 1.0, 6.0, ((0, 8), (1, 16)))
    surface_factor = centred(key_of[9], (NRHS, NSURF), (4 * NRHS) ** -0.5, 0.125, ((1, 16),))
    return {"rhs": rhs, "couple_prev": couple_prev, "diag_inverse": diag_inverse, "coupling": coupling, "pair_block": pair_block, "pair_tile": pair_tile, "pair_count": pair_count, "owner_slot": owner_slot, "schur": schur, "surface_factor": surface_factor}


def owner_update(blocks, tiles, count, tiles_data, sol_blocks):
    hi = lax.Precision.HIGHEST
    picked = jnp.take(sol_blocks, blocks, axis=1)
    product = jnp.einsum("kib,rkb->kir", tiles_data.astype(jnp.float32), picked.astype(jnp.float32), precision=hi)
    live = jnp.arange(KCAP) < count
    weight = ((tiles[None, :] == jnp.arange(TPD)[:, None]) & live[None, :]).astype(jnp.float32)
    return jnp.einsum("tk,kir->tir", weight, product, precision=hi).astype(jnp.bfloat16)


def reference(rhs, couple_prev, diag_inverse, coupling, pair_block, pair_tile, pair_count, owner_slot, schur, surface_factor):
    hi = lax.Precision.HIGHEST
    pieces = []
    previous = None
    for block_row in range(N_ROW):
        right = rhs[:, block_row * NB:(block_row + 1) * NB]
        lower = couple_prev[block_row * NB:(block_row + 1) * NB]
        inverse = diag_inverse[block_row * NB:(block_row + 1) * NB]
        if block_row > 0:
            right = right - jnp.dot(previous, lower, precision=hi, preferred_element_type=jnp.float32)
        previous = jnp.dot(right, inverse, precision=hi, preferred_element_type=jnp.float32)
        pieces.append(previous)
    solution = jnp.concatenate(pieces, axis=1).astype(jnp.bfloat16)
    sol_blocks = solution.reshape(NRHS, NS // BLK, BLK)
    owners = N_ROW * N_COL

    def one_owner(items):
        return owner_update(items[0], items[1], items[2], items[3], sol_blocks)

    update = lax.map(one_owner, (pair_block.reshape(owners, KCAP), pair_tile.reshape(owners, KCAP), pair_count, coupling.reshape(owners, KCAP, TILE, BLK)))
    update = update.reshape(N_ROW, TPR, TILE, NRHS)

    def one_group(items):
        rows_all, slots, slab = items
        rows = jnp.take(rows_all, slots, axis=0).reshape(SR, NRHS)
        change = jnp.dot(rows, surface_factor, preferred_element_type=jnp.float32)
        return (slab.astype(jnp.float32) - change).astype(jnp.bfloat16)

    result = lax.map(one_group, (update, owner_slot, schur.reshape(N_ROW, SR, NSURF)))
    return result.reshape(N_ROW * SR, NSURF)
```

```python
import jax
import jax.numpy as jnp
from jax import lax
from jax.experimental import pallas as pl
from jax.experimental.pallas import tpu as pltpu
from jax.sharding import PartitionSpec as P

NB = 1024
BLK = 128
TILE = 16
TPD = 3
KCAP = 12
TPR = 48
SR = 768
NRHS = 512
N_ROW = 8
N_COL = 16
COLS = NRHS // N_COL
PER = NB // BLK
SIDE = 4
BF = jnp.bfloat16
F32 = jnp.float32


def split(value):
    high = value.astype(BF)
    return high, (value - high.astype(F32)).astype(BF)


def mm(left, right):
    return jnp.dot(left, right, preferred_element_type=F32)


def prep_body(rhs_ref, e_ref, g_ref, y_ref, f_ref, e_high, e_low):
    @pl.when(pl.program_id(0) == 0)
    def _():
        high, low = split(e_ref[...])
        e_high[...] = high
        e_low[...] = low

    g_high, g_low = split(g_ref[...])
    r_high, r_low = split(rhs_ref[...])
    y_ref[...] = mm(r_high, g_high) + mm(r_high, g_low) + mm(r_low, g_high)
    change = mm(e_high[...], g_high) + mm(e_high[...], g_low) + mm(e_low[...], g_high)
    f_ref[...] = (-change).astype(BF)


def prep(rhs, lower, inverse):
    wide = 256
    return pl.pallas_call(
        prep_body,
        grid=(NB // wide,),
        in_specs=[
            pl.BlockSpec((COLS, NB), lambda i: (0, 0)),
            pl.BlockSpec((NB, NB), lambda i: (0, 0)),
            pl.BlockSpec((NB, wide), lambda i: (0, i)),
        ],
        out_specs=[
            pl.BlockSpec((COLS, wide), lambda i: (0, i)),
            pl.BlockSpec((NB, wide), lambda i: (0, i)),
        ],
        out_shape=[
            jax.ShapeDtypeStruct((COLS, NB), F32),
            jax.ShapeDtypeStruct((NB, NB), BF),
        ],
        scratch_shapes=[pltpu.VMEM((NB, NB), BF), pltpu.VMEM((NB, NB), BF)],
        compiler_params=pltpu.CompilerParams(vmem_limit_bytes=24 << 20),
        name="prep",
    )(rhs, lower, inverse)


def build_body(blocks, tiles, slots, owners, c0, c1, c2, c3, out_ref, place):
    out_ref[...] = jnp.zeros_like(out_ref)

    @pl.loop(0, TPR)
    def _(i):
        place[slots[i]] = i

    for part, ref in enumerate((c0, c1, c2, c3)):

        @pl.loop(0, SIDE)
        def _(z):
            owner = owners[part * SIDE + z]
            for k in range(KCAP):
                at = (part * SIDE + z) * KCAP + k
                row = pl.multiple_of(place[owner * TPD + tiles[at]] * TILE, TILE)
                block = blocks[at]
                lane = pl.multiple_of((block % PER) * BLK, BLK)
                spot = (block // PER, pl.ds(row, TILE), pl.ds(lane, BLK))
                out_ref[spot] = out_ref[spot] + ref[z, k]


def build(blocks, tiles, slots, owners, parts):
    whole = pl.BlockSpec(memory_space=pltpu.VMEM)
    return pl.pallas_call(
        build_body,
        grid_spec=pltpu.PrefetchScalarGridSpec(
            num_scalar_prefetch=4,
            grid=(1,),
            in_specs=[pl.BlockSpec((SIDE, KCAP + 1, TILE, BLK), lambda i, *_: (0, 0, 0, 0))] * 4,
            out_specs=pl.BlockSpec((N_ROW, SR, NB), lambda i, *_: (0, 0, 0), pipeline_mode=pl.Buffered(1)),
            scratch_shapes=[pltpu.SMEM((TPR,), jnp.int32)],
        ),
        out_shape=jax.ShapeDtypeStruct((N_ROW, SR, NB), BF),
        compiler_params=pltpu.CompilerParams(vmem_limit_bytes=24 << 20),
        name="build",
    )(blocks, tiles, slots, owners, *parts)


def products_body(core, c_ref, own_ref, other_ref, last_own, last_other, out_ref, chunk, sems):
    mine = core[0]

    def fetch(group, slot):
        return pltpu.make_async_copy(c_ref.at[group], chunk.at[slot], sems.at[slot])

    sources = []
    for pair in range(4):
        for side in range(2):
            sources.append((pair, side))
    groups = [2 * pair + (mine if side == 0 else 1 - mine) for pair, side in sources]
    fetch(groups[0], 0).start()
    total = None
    for at, (pair, side) in enumerate(sources):
        if at + 1 < len(sources):
            fetch(groups[at + 1], (at + 1) % 2).start()
        fetch(groups[at], at % 2).wait()
        if pair < 3:
            x = (own_ref if side == 0 else other_ref)[pair]
        else:
            x = (last_own if side == 0 else last_other)[...]
        part = lax.dot_general(chunk[at % 2], x, (((1,), (1,)), ((), ())), preferred_element_type=F32)
        total = part if total is None else total + part
    out_ref[...] = total.T.astype(BF)


def products(core, dense, own, other, last_own, last_other):
    vmem = pl.BlockSpec(memory_space=pltpu.VMEM)
    return pl.pallas_call(
        products_body,
        in_specs=[pl.BlockSpec(memory_space=pltpu.SMEM), pl.BlockSpec(memory_space=pl.ANY), vmem, vmem, vmem, vmem],
        out_specs=vmem,
        out_shape=jax.ShapeDtypeStruct((COLS, SR), BF),
        scratch_shapes=[pltpu.VMEM((2, SR, NB), BF), pltpu.SemaphoreType.DMA((2,))],
        compiler_params=pltpu.CompilerParams(vmem_limit_bytes=16 << 20),
        name="products",
    )(core, dense, own, other, last_own, last_other)


def final_body(owners, w0, w1, w2, w3, s_ref, schur_ref, out_ref, stacked, turned):
    @pl.when(pl.program_id(0) == 0)
    def _():
        for part, ref in enumerate((w0, w1, w2, w3)):
            for z in range(SIDE):
                at = pl.multiple_of(owners[part * SIDE + z] * COLS, COLS)
                stacked[pl.ds(at, COLS), :] = ref[z]
        turned[...] = stacked[...].T

    change = mm(turned[...], s_ref[...])
    out_ref[...] = (schur_ref[...].astype(F32) - change).astype(BF)


def final(owners, parts, factor, schur):
    wide = 512
    width = schur.shape[1]
    piece = pl.BlockSpec((SIDE, COLS, SR), lambda i, *_: (0, 0, 0))
    return pl.pallas_call(
        final_body,
        grid_spec=pltpu.PrefetchScalarGridSpec(
            num_scalar_prefetch=1,
            grid=(width // wide,),
            in_specs=[piece] * 4
            + [
                pl.BlockSpec((NRHS, wide), lambda i, *_: (0, i)),
                pl.BlockSpec((SR, wide), lambda i, *_: (0, i)),
            ],
            out_specs=pl.BlockSpec((SR, wide), lambda i, *_: (0, i)),
            scratch_shapes=[pltpu.VMEM((NRHS, SR), BF), pltpu.VMEM((SR, NRHS), BF)],
        ),
        out_shape=jax.ShapeDtypeStruct(schur.shape, BF),
        compiler_params=pltpu.CompilerParams(vmem_limit_bytes=24 << 20),
        name="final",
    )(owners, *parts, factor, schur)


def gather_cols(value):
    def turned(v, dx, dz):
        pairs = [(x * SIDE + z, (x + dx) % SIDE * SIDE + (z + dz) % SIDE) for x in range(SIDE) for z in range(SIDE)]
        return lax.ppermute(v, "col", pairs)

    near = jnp.stack([value] + [turned(value, 0, dz) for dz in (1, 2, 3)])
    return [near] + [turned(near, dx, 0) for dx in (1, 2, 3)]


def chip_move(value, pairs):
    return lax.ppermute(value, "row", [(2 * a + c, 2 * b + c) for a, b in pairs for c in (0, 1)])


def spread(value, chip, j):
    up, down, far = (j + 1) % 4, (j - 1) % 4, (j + 2) % 4
    a = chip_move(value, [(j, up)])
    b = chip_move(value, [(j, down)])
    f = chip_move(a, [(up, far)])
    return jnp.where(chip == j, value, a + b + f)


def swap_cores(value):
    return lax.ppermute(value, "row", [(i, i ^ 1) for i in range(N_ROW)])


def shards(rhs, couple_prev, diag_inverse, coupling, pair_block, pair_tile, pair_count, owner_slot, schur, surface_factor):
    row = lax.axis_index("row")
    col = lax.axis_index("col")
    chip, core = row // 2, row % 2
    live = jnp.arange(KCAP) < pair_count[0]
    tiles_data = jnp.where(live[:, None, None], coupling, jnp.zeros((), BF))
    info = jnp.stack([pair_block, pair_tile]).astype(BF)
    info = jnp.pad(info, ((0, TILE - 2), (0, BLK - KCAP)))
    parts = gather_cols(jnp.concatenate([tiles_data, info[None]], axis=0))
    codes = jnp.stack([p[:, KCAP, :2, :KCAP] for p in parts]).astype(jnp.int32)
    blocks = codes[:, :, 0].reshape(-1)
    tiles = codes[:, :, 1].reshape(-1)
    steps = jnp.arange(SIDE, dtype=jnp.int32)
    owners = ((col // SIDE - steps[:, None]) % SIDE * SIDE + (col % SIDE - steps[None, :]) % SIDE).reshape(-1)
    dense = build(blocks, tiles, owner_slot[0], owners, parts)

    x, f = prep(rhs, couple_prev, diag_inverse)
    sent = x.astype(BF)
    lines = []
    for step in range(N_ROW - 1):
        before = lax.ppermute(sent, "row", [(step, step + 1)])
        x = x + mm(before, f)
        sent = x.astype(BF)
        if step % 2 == 0:
            lines.append(spread(sent, chip, step // 2))
    own = jnp.stack(lines[:3])
    other = swap_cores(own)
    last_other = swap_cores(lines[3])
    update = products(core[None], dense, own, other, lines[3], last_other)
    return final(owners, gather_cols(update), surface_factor, schur)


def solution(mesh):
    placed = (
        P("col", "row"),
        P("row", None),
        P("row", None),
        P(("row", "col"), None, None),
        P(("row", "col")),
        P(("row", "col")),
        P(("row", "col")),
        P("row", None),
        P("row", "col"),
        P(None, "col"),
    )
    return jax.shard_map(shards, mesh=mesh, in_specs=placed, out_specs=P("row", "col"), check_vma=False)
```

```python
import jax
import jax.numpy as jnp
from jax import lax
from jax.experimental import pallas as pl
from jax.experimental.pallas import tpu as pltpu
from jax.sharding import PartitionSpec as P

NB = 1024
BLK = 128
TILE = 16
TPD = 3
KCAP = 12
TPR = 48
SR = 768
NRHS = 512
N_ROW = 8
N_COL = 16
COLS = NRHS // N_COL
PER = NB // BLK
SIDE = 4
CHUNKS = 4
BF = jnp.bfloat16
F32 = jnp.float32


def split(value):
    high = value.astype(BF)
    return high, (value - high.astype(F32)).astype(BF)


def in_hbm(value):
    return pltpu.with_memory_space_constraint(value, pltpu.HBM)


def mm(left, right):
    return jnp.dot(left, right, preferred_element_type=F32)


def vmem():
    return pl.BlockSpec(memory_space=pltpu.VMEM)


def smem():
    return pl.BlockSpec(memory_space=pltpu.SMEM)


def small(limit):
    return pltpu.CompilerParams(vmem_limit_bytes=limit << 20)


def prep_body(rhs_ref, e_hbm, g_hbm, y_ref, sent_ref, high_ref, low_ref, e_in, g_in, g_high, g_low, sems):
    rows = NB // CHUNKS

    def fetch(at):
        source, target = (g_hbm, g_in) if at < CHUNKS else (e_hbm, e_in)
        piece = pl.ds(at % CHUNKS * rows, rows)
        return pltpu.make_async_copy(source.at[piece], target.at[piece], sems.at[at])

    for at in range(2 * CHUNKS):
        fetch(at).start()
    for at in range(CHUNKS):
        piece = pl.ds(at * rows, rows)
        fetch(at).wait()
        g_high[piece], g_low[piece] = split(g_in[piece])
    r_high, r_low = split(rhs_ref[...])
    y = mm(r_high, g_high[...]) + mm(r_high, g_low[...]) + mm(r_low, g_high[...])
    y_ref[...] = y
    sent_ref[...] = y.astype(BF)
    for at in range(CHUNKS):
        piece = pl.ds(at * rows, rows)
        fetch(CHUNKS + at).wait()
        high, low = split(-e_in[piece])
        change = mm(high, g_high[...]) + mm(high, g_low[...]) + mm(low, g_high[...])
        high_ref[piece], low_ref[piece] = split(change)


def prep(rhs, lower, inverse):
    hbm = pl.BlockSpec(memory_space=pltpu.HBM)
    square = jax.ShapeDtypeStruct((NB, NB), BF)
    return pl.pallas_call(
        prep_body,
        in_specs=[vmem(), hbm, hbm],
        out_specs=[vmem()] * 4,
        out_shape=[jax.ShapeDtypeStruct((COLS, NB), F32), jax.ShapeDtypeStruct((COLS, NB), BF), square, square],
        scratch_shapes=[
            pltpu.VMEM((NB, NB), F32),
            pltpu.VMEM((NB, NB), F32),
            pltpu.VMEM((NB, NB), BF),
            pltpu.VMEM((NB, NB), BF),
            pltpu.SemaphoreType.DMA((2 * CHUNKS,)),
        ],
        compiler_params=small(20),
        name="prep",
    )(rhs, in_hbm(lower), in_hbm(inverse))


def advance(step, y, sent, before, high, low):
    def body(sent_ref, y_ref, before_ref, high_ref, low_ref, out_ref):
        @pl.when(lax.axis_index("row") == step + 1)
        def _():
            moved = before_ref[...]
            out_ref[...] = (y_ref[...] + mm(moved, high_ref[...]) + mm(moved, low_ref[...])).astype(BF)

    return pl.pallas_call(
        body,
        in_specs=[vmem()] * 5,
        out_specs=vmem(),
        out_shape=jax.ShapeDtypeStruct((COLS, NB), BF),
        input_output_aliases={0: 0},
        compiler_params=small(4),
        name=f"advance{step}",
    )(sent, y, before, high, low)


def pack_body(blocks, tiles, count, coupling_ref, out_ref):
    lane = lax.broadcasted_iota(jnp.int32, (TILE, BLK), 1)
    info = jnp.zeros((TILE, BLK), jnp.int32)
    for k in range(KCAP):
        info = jnp.where(lane == k, blocks[k], info)
        info = jnp.where(lane == k + TILE, tiles[k], info)
        tile = coupling_ref[k]
        out_ref[k] = jnp.where(k < count[0], tile, jnp.zeros_like(tile))
    out_ref[KCAP] = info.astype(F32).astype(BF)


def pack(coupling, blocks, tiles, count):
    return pl.pallas_call(
        pack_body,
        in_specs=[smem()] * 3 + [vmem()],
        out_specs=vmem(),
        out_shape=jax.ShapeDtypeStruct((KCAP + 1, TILE, BLK), BF),
        compiler_params=small(2),
        name="pack",
    )(blocks, tiles, count, coupling)


def came_from(dx, dz):
    col = lax.axis_index("col")
    return (col // SIDE - dx) % SIDE * SIDE + (col % SIDE - dz) % SIDE


def build_body(slots, c0, c1, c2, c3, out_ref, place, info, codes, sem):
    parts = (c0, c1, c2, c3)
    for part, ref in enumerate(parts):
        for z in range(SIDE):
            info[pl.ds(part * SIDE + z, 1)] = ref[z, KCAP].astype(F32)[:1].astype(jnp.int32)
    move = pltpu.make_async_copy(info, codes, sem)
    move.start()
    out_ref[...] = jnp.zeros_like(out_ref)

    @pl.loop(0, TPR)
    def _(i):
        place[slots[0, i]] = i

    move.wait()
    for part, ref in enumerate(parts):

        @pl.loop(0, SIDE)
        def _(z):
            at = part * SIDE + z
            first = came_from(part, z) * TPD
            for k in range(KCAP):
                block = codes[at, k]
                row = pl.multiple_of(place[first + codes[at, k + TILE]] * TILE, TILE)
                lane = pl.multiple_of(block % PER * BLK, BLK)
                spot = (block // PER, pl.ds(row, TILE), pl.ds(lane, BLK))
                out_ref[spot] = out_ref[spot] + ref[z, k]


def build(slots, parts):
    return pl.pallas_call(
        build_body,
        in_specs=[smem()] + [vmem()] * 4,
        out_specs=vmem(),
        scratch_shapes=[
            pltpu.SMEM((TPR,), jnp.int32),
            pltpu.VMEM((N_COL, BLK), jnp.int32),
            pltpu.SMEM((N_COL, BLK), jnp.int32),
            pltpu.SemaphoreType.DMA(()),
        ],
        out_shape=jax.ShapeDtypeStruct((N_ROW, SR, NB), BF),
        compiler_params=small(4),
        name="build",
    )(slots, *parts)


def line_sum(other, c_ref, x_ref):
    row = lax.axis_index("row")
    chip, core = row // 2, row % 2
    side = 1 - core if other else core
    total = None
    for k in range(SIDE):
        group = 2 * ((chip - k) % SIDE) + side
        part = lax.dot_general(c_ref[group], x_ref[k], (((1,), (1,)), ((), ())), preferred_element_type=F32)
        total = part if total is None else total + part
    return total


def own_body(c_ref, x_ref, out_ref):
    out_ref[...] = line_sum(False, c_ref, x_ref)


def other_body(c_ref, x_ref, sum_ref, out_ref):
    out_ref[...] = (sum_ref[...] + line_sum(True, c_ref, x_ref)).T.astype(BF)


def products_own(dense, line):
    return pl.pallas_call(
        own_body,
        in_specs=[vmem()] * 2,
        out_specs=vmem(),
        out_shape=jax.ShapeDtypeStruct((SR, COLS), F32),
        compiler_params=small(4),
        name="products_own",
    )(dense, line)


def products_other(dense, line, sums):
    return pl.pallas_call(
        other_body,
        in_specs=[vmem()] * 3,
        out_specs=vmem(),
        out_shape=jax.ShapeDtypeStruct((COLS, SR), BF),
        compiler_params=small(4),
        name="products_other",
    )(dense, line, sums)


def final_body(w0, w1, w2, w3, s_ref, schur_ref, out_ref, stacked, turned):
    wide = out_ref.shape[1]

    @pl.when(pl.program_id(0) == 0)
    def _():
        for part, ref in enumerate((w0, w1, w2, w3)):
            for z in range(SIDE):
                at = pl.multiple_of(came_from(part, z) * COLS, COLS)
                stacked[pl.ds(at, COLS), :] = ref[z]
        turned[...] = stacked[...].T

    at = pl.ds(pl.multiple_of(pl.program_id(0) * wide, wide), wide)
    change = mm(turned[...], s_ref[:, at])
    out_ref[...] = (schur_ref[:, at].astype(F32) - change).astype(BF)


def final(parts, factor, schur):
    wide = 512
    width = schur.shape[1]
    return pl.pallas_call(
        final_body,
        grid=(width // wide,),
        in_specs=[vmem()] * 6,
        out_specs=pl.BlockSpec((SR, wide), lambda i: (0, i)),
        scratch_shapes=[pltpu.VMEM((NRHS, SR), BF), pltpu.VMEM((SR, NRHS), BF)],
        out_shape=jax.ShapeDtypeStruct(schur.shape, BF),
        compiler_params=small(10),
        name="final",
    )(*parts, factor, schur)


def turned_cols(value, dx, dz):
    pairs = [(x * SIDE + z, (x + dx) % SIDE * SIDE + (z + dz) % SIDE) for x in range(SIDE) for z in range(SIDE)]
    return lax.ppermute(value, "col", pairs)


def gather_near(value):
    return [value] + [turned_cols(value, 0, dz) for dz in (1, 2, 3)]


def gather_far(near):
    return [near] + [turned_cols(near, dx, 0) for dx in (1, 2, 3)]


def gather_chips(value):
    def moved(k):
        return lax.ppermute(value, "row", [(2 * a + c, 2 * ((a + k) % SIDE) + c) for a in range(SIDE) for c in (0, 1)])

    return jnp.stack([value] + [moved(k) for k in (1, 2, 3)])


def swap_cores(value):
    return lax.ppermute(value, "row", [(i, i ^ 1) for i in range(N_ROW)])


def after(value, earlier):
    return lax.optimization_barrier((value, earlier))[0]


def shards(rhs, couple_prev, diag_inverse, coupling, pair_block, pair_tile, pair_count, owner_slot, schur, surface_factor):
    y, sent, high, low = prep(rhs, couple_prev, diag_inverse)
    near = parts = dense = None
    for step in range(N_ROW - 1):
        before = lax.ppermute(sent, "row", [(step, step + 1)])
        if step == 1:
            packed = pack(after(coupling, sent), pair_block, pair_tile, pair_count)
        if step == 2:
            near = gather_near(after(packed, sent))
        if step == 3:
            near = jnp.stack([near[0]] + [after(part, sent) for part in near[1:]])
            parts = gather_far(near)
            before = after(before, near)
        if step == 6:
            dense = build(owner_slot, [parts[0]] + [after(part, sent) for part in parts[1:]])
            before = after(before, dense)
        sent = advance(step, y, sent, before, high, low)
    line = gather_chips(sent)
    other = swap_cores(line)
    update = products_other(dense, other, products_own(dense, line))
    return final(gather_far(jnp.stack(gather_near(update))), surface_factor, schur)


def solution(mesh):
    placed = (
        P("col", "row"),
        P("row", None),
        P("row", None),
        P(("row", "col"), None, None),
        P(("row", "col")),
        P(("row", "col")),
        P(("row", "col")),
        P("row", None),
        P("row", "col"),
        P(None, "col"),
    )
    return jax.shard_map(shards, mesh=mesh, in_specs=placed, out_specs=P("row", "col"), check_vma=False)
```

```python
import jax
import jax.numpy as jnp
from jax import lax
from jax.experimental import pallas as pl
from jax.experimental.pallas import tpu as pltpu
from jax.sharding import PartitionSpec as P

NB = 1024
BLK = 128
TILE = 16
TPD = 3
KCAP = 12
TPR = 48
SR = 768
NRHS = 512
N_ROW = 8
N_COL = 16
COLS = NRHS // N_COL
PER = NB // BLK
SIDE = 4
CHUNKS = 4
BF = jnp.bfloat16
F32 = jnp.float32


def split(value):
    high = value.astype(BF)
    return high, (value - high.astype(F32)).astype(BF)


def in_hbm(value):
    return pltpu.with_memory_space_constraint(value, pltpu.HBM)


def mm(left, right):
    return jnp.dot(left, right, preferred_element_type=F32)


def vmem():
    return pl.BlockSpec(memory_space=pltpu.VMEM)


def smem():
    return pl.BlockSpec(memory_space=pltpu.SMEM)


def small(limit):
    return pltpu.CompilerParams(vmem_limit_bytes=limit << 20)


def start_copies(source, target, sems, first, count, rows, skip=0):
    moves = []
    for at in range(count):
        piece = pl.ds(skip + at * rows, rows)
        moves.append(pltpu.make_async_copy(source.at[piece], target.at[pl.ds(at * rows, rows)], sems.at[first + at]))
        moves[-1].start()
    return moves


def change_rows(e_in, piece, g_high, g_low):
    high, low = split(-e_in[piece])
    return split(mm(high, g_high[...]) + mm(high, g_low[...]) + mm(low, g_high[...]))


def first_body(rhs_ref, e_hbm, g_hbm, y_ref, sent_ref, high_ref, low_ref, g_high, g_low, e_in, g_in, sems):
    rows = NB // CHUNKS
    load_g = start_copies(g_hbm, g_in, sems, 0, CHUNKS, rows)
    load_e = start_copies(e_hbm, e_in, sems, CHUNKS, CHUNKS // 2, rows)
    for at, move in enumerate(load_g):
        piece = pl.ds(at * rows, rows)
        move.wait()
        g_high[piece], g_low[piece] = split(g_in[piece])
    r_high, r_low = split(rhs_ref[...])
    y = mm(r_high, g_high[...]) + mm(r_high, g_low[...]) + mm(r_low, g_high[...])
    y_ref[...] = y
    sent_ref[...] = y.astype(BF)
    for at, move in enumerate(load_e):
        piece = pl.ds(at * rows, rows)
        move.wait()
        high_ref[piece], low_ref[piece] = change_rows(e_in, piece, g_high, g_low)


def second_body(e_hbm, g_high, g_low, high_ref, low_ref, e_in, sems):
    rows = NB // CHUNKS // 2
    for at, move in enumerate(start_copies(e_hbm, e_in, sems, 0, CHUNKS, rows, NB // 2)):
        piece = pl.ds(at * rows, rows)
        move.wait()
        high_ref[piece], low_ref[piece] = change_rows(e_in, piece, g_high, g_low)


def hbm():
    return pl.BlockSpec(memory_space=pltpu.HBM)


def shape(rows, kind=BF):
    return jax.ShapeDtypeStruct((rows, NB), kind)


def prep_first(rhs, lower, inverse):
    return pl.pallas_call(
        first_body,
        in_specs=[vmem(), hbm(), hbm()],
        out_specs=[vmem()] * 6,
        out_shape=[shape(COLS, F32), shape(COLS), shape(NB // 2), shape(NB // 2), shape(NB), shape(NB)],
        scratch_shapes=[
            pltpu.VMEM((NB // 2, NB), F32),
            pltpu.VMEM((NB, NB), F32),
            pltpu.SemaphoreType.DMA((2 * CHUNKS,)),
        ],
        compiler_params=small(14),
        name="prep_first",
    )(rhs, in_hbm(lower), in_hbm(inverse))


def prep_second(lower, g_high, g_low):
    return pl.pallas_call(
        second_body,
        in_specs=[hbm(), vmem(), vmem()],
        out_specs=[vmem()] * 2,
        out_shape=[shape(NB // 2)] * 2,
        scratch_shapes=[pltpu.VMEM((NB // 2, NB), F32), pltpu.SemaphoreType.DMA((CHUNKS,))],
        compiler_params=small(10),
        name="prep_second",
    )(in_hbm(lower), g_high, g_low)


def times(left, refs):
    half = NB // 2
    upper, lower = left[:, :half], left[:, half:]
    return mm(upper, refs[0][...]) + mm(upper, refs[1][...]) + mm(lower, refs[2][...]) + mm(lower, refs[3][...])


def pair_rows(moved, halves):
    def body(moved_ref, f0, f1, f2, f3, high_ref, low_ref):
        @pl.when(lax.axis_index("row") % 2 == 1)
        def _():
            high_ref[...], low_ref[...] = split(times(moved_ref[...], (f0, f1, f2, f3)))

    return pl.pallas_call(
        body,
        in_specs=[vmem()] * 5,
        out_specs=[vmem()] * 2,
        out_shape=[shape(NB // 2)] * 2,
        compiler_params=small(12),
        name="pair_rows",
    )(moved, *halves)


def join(y, sent, moved, halves):
    def body(y_ref, sent_ref, moved_ref, f0, f1, f2, f3, base_ref, out_ref):
        @pl.when(lax.axis_index("row") % 2 == 1)
        def _():
            base = y_ref[...] + times(moved_ref[...], (f0, f1, f2, f3))
            base_ref[...] = base
            out_ref[...] = base.astype(BF)

    return pl.pallas_call(
        body,
        in_specs=[vmem()] * 7,
        out_specs=[vmem()] * 2,
        out_shape=[shape(COLS, F32), shape(COLS)],
        input_output_aliases={0: 0, 1: 1},
        compiler_params=small(4),
        name="join",
    )(y, sent, moved, *halves)


def advance(row, base, sent, moved, pairs):
    def body(sent_ref, base_ref, moved_ref, h0, h1, h2, h3, out_ref):
        @pl.when(lax.axis_index("row") == row)
        def _():
            out_ref[...] = (base_ref[...] + times(moved_ref[...], (h0, h1, h2, h3))).astype(BF)

    return pl.pallas_call(
        body,
        in_specs=[vmem()] * 7,
        out_specs=vmem(),
        out_shape=shape(COLS),
        input_output_aliases={0: 0},
        compiler_params=small(4),
        name=f"advance{row}",
    )(sent, base, moved, *pairs)


def finish(base, sent, moved, moved_even, pairs, halves):
    def body(sent_ref, base_ref, moved_ref, even_ref, h0, h1, h2, h3, f0, f1, f2, f3, out_ref):
        row = lax.axis_index("row")

        @pl.when(row == N_ROW - 1)
        def _():
            out_ref[...] = (base_ref[...] + times(moved_ref[...], (h0, h1, h2, h3))).astype(BF)

        @pl.when((row % 2 == 0) & (row > 0))
        def _():
            out_ref[...] = (base_ref[...] + times(even_ref[...], (f0, f1, f2, f3))).astype(BF)

    return pl.pallas_call(
        body,
        in_specs=[vmem()] * 12,
        out_specs=vmem(),
        out_shape=shape(COLS),
        input_output_aliases={0: 0},
        compiler_params=small(4),
        name="finish",
    )(sent, base, moved, moved_even, *pairs, *halves)


def pack_body(blocks, tiles, count, coupling_ref, out_ref):
    lane = lax.broadcasted_iota(jnp.int32, (TILE, BLK), 1)
    info = jnp.zeros((TILE, BLK), jnp.int32)
    for k in range(KCAP):
        info = jnp.where(lane == k, blocks[k], info)
        info = jnp.where(lane == k + TILE, tiles[k], info)
        tile = coupling_ref[k]
        out_ref[k] = jnp.where(k < count[0], tile, jnp.zeros_like(tile))
    out_ref[KCAP] = info.astype(F32).astype(BF)


def pack(coupling, blocks, tiles, count):
    return pl.pallas_call(
        pack_body,
        in_specs=[smem()] * 3 + [vmem()],
        out_specs=vmem(),
        out_shape=jax.ShapeDtypeStruct((KCAP + 1, TILE, BLK), BF),
        compiler_params=small(2),
        name="pack",
    )(blocks, tiles, count, coupling)


def came_from(dx, dz):
    col = lax.axis_index("col")
    return (col // SIDE - dx) % SIDE * SIDE + (col % SIDE - dz) % SIDE


def clear():
    def body(out_ref):
        out_ref[...] = jnp.zeros_like(out_ref)

    return pl.pallas_call(
        body,
        out_specs=vmem(),
        out_shape=jax.ShapeDtypeStruct((N_ROW, SR, NB), BF),
        compiler_params=small(2),
        name="clear",
    )()


def build_body(slots, c0, c1, c2, c3, cleared, out_ref, place, info, codes, sem):
    parts = (c0, c1, c2, c3)
    for part, ref in enumerate(parts):
        for z in range(SIDE):
            info[pl.ds(part * SIDE + z, 1)] = ref[z, KCAP].astype(F32)[:1].astype(jnp.int32)
    move = pltpu.make_async_copy(info, codes, sem)
    move.start()

    @pl.loop(0, TPR)
    def _(i):
        place[slots[0, i]] = i

    move.wait()
    for part, ref in enumerate(parts):

        @pl.loop(0, SIDE)
        def _(z):
            at = part * SIDE + z
            first = came_from(part, z) * TPD
            for k in range(KCAP):
                block = codes[at, k]
                row = pl.multiple_of(place[first + codes[at, k + TILE]] * TILE, TILE)
                lane = pl.multiple_of(block % PER * BLK, BLK)
                spot = (block // PER, pl.ds(row, TILE), pl.ds(lane, BLK))
                out_ref[spot] = out_ref[spot] + ref[z, k]


def build(slots, parts, cleared):
    return pl.pallas_call(
        build_body,
        in_specs=[smem()] + [vmem()] * 5,
        out_specs=vmem(),
        input_output_aliases={5: 0},
        scratch_shapes=[
            pltpu.SMEM((TPR,), jnp.int32),
            pltpu.VMEM((N_COL, BLK), jnp.int32),
            pltpu.SMEM((N_COL, BLK), jnp.int32),
            pltpu.SemaphoreType.DMA(()),
        ],
        out_shape=jax.ShapeDtypeStruct((N_ROW, SR, NB), BF),
        compiler_params=small(4),
        name="build",
    )(slots, *parts, cleared)


def line_sum(other, c_ref, x_ref):
    row = lax.axis_index("row")
    chip, core = row // 2, row % 2
    side = 1 - core if other else core
    total = None
    for k in range(SIDE):
        group = 2 * ((chip - k) % SIDE) + side
        part = lax.dot_general(c_ref[group], x_ref[k], (((1,), (1,)), ((), ())), preferred_element_type=F32)
        total = part if total is None else total + part
    return total


def own_body(c_ref, x_ref, out_ref):
    out_ref[...] = line_sum(False, c_ref, x_ref)


def other_body(c_ref, x_ref, sum_ref, out_ref):
    out_ref[...] = (sum_ref[...] + line_sum(True, c_ref, x_ref)).T.astype(BF)


def products_own(dense, line):
    return pl.pallas_call(
        own_body,
        in_specs=[vmem()] * 2,
        out_specs=vmem(),
        out_shape=jax.ShapeDtypeStruct((SR, COLS), F32),
        compiler_params=small(4),
        name="products_own",
    )(dense, line)


def products_other(dense, line, sums):
    return pl.pallas_call(
        other_body,
        in_specs=[vmem()] * 3,
        out_specs=vmem(),
        out_shape=jax.ShapeDtypeStruct((COLS, SR), BF),
        compiler_params=small(4),
        name="products_other",
    )(dense, line, sums)


def final_body(w0, w1, w2, w3, s_ref, schur_ref, out_hbm, stacked, turned, out, sems):
    tall, wide = 256, 1024
    for part, ref in enumerate((w0, w1, w2, w3)):
        for z in range(SIDE):
            at = pl.multiple_of(came_from(part, z) * COLS, COLS)
            stacked[pl.ds(at, COLS), :] = ref[z]
    moves = []
    for m in range(SR // tall):
        rows = pl.ds(m * tall, tall)
        turned[rows, :] = stacked[:, rows].T
        for n in range(schur_ref.shape[1] // wide):
            cols = pl.ds(n * wide, wide)
            slot = len(moves) % 4
            if len(moves) >= 4:
                moves[-4].wait()
            change = mm(turned[rows, :], s_ref[:, cols])
            out[slot] = (schur_ref[rows, cols].astype(F32) - change).astype(BF)
            moves.append(pltpu.make_async_copy(out.at[slot], out_hbm.at[rows, cols], sems.at[slot]))
            moves[-1].start()
    for move in moves[-4:]:
        move.wait()


def final(parts, factor, schur):
    return pl.pallas_call(
        final_body,
        in_specs=[vmem()] * 6,
        out_specs=hbm(),
        scratch_shapes=[
            pltpu.VMEM((NRHS, SR), BF),
            pltpu.VMEM((SR, NRHS), BF),
            pltpu.VMEM((4, 256, 1024), BF),
            pltpu.SemaphoreType.DMA((4,)),
        ],
        out_shape=jax.ShapeDtypeStruct(schur.shape, BF),
        compiler_params=small(10),
        name="final",
    )(*parts, factor, schur)


def turned_cols(value, dx, dz):
    pairs = [(x * SIDE + z, (x + dx) % SIDE * SIDE + (z + dz) % SIDE) for x in range(SIDE) for z in range(SIDE)]
    return lax.ppermute(value, "col", pairs)


def gather_near(value):
    return [value] + [turned_cols(value, 0, dz) for dz in (1, 2, 3)]


def gather_far(near):
    return [near] + [turned_cols(near, dx, 0) for dx in (1, 2, 3)]


def gather_chips(value, first):
    def moved(k):
        return lax.ppermute(value, "row", [(2 * a + c, 2 * ((a + k) % SIDE) + c) for a in range(SIDE) for c in (0, 1)])

    return jnp.stack([value] + [after(moved(k), first) for k in (1, 2, 3)])


def swap_cores(value):
    return lax.ppermute(value, "row", [(i, i ^ 1) for i in range(N_ROW)])


def after(value, earlier):
    return lax.optimization_barrier((value, earlier))[0]


def shards(rhs, couple_prev, diag_inverse, coupling, pair_block, pair_tile, pair_count, owner_slot, schur, surface_factor):
    def hop(value, pairs):
        return lax.ppermute(value, "row", pairs)

    within = [(2 * j, 2 * j + 1) for j in range(SIDE)]
    packed = pack(coupling, pair_block, pair_tile, pair_count)
    near = gather_near(packed)
    y, sent, f0, f1, g_high, g_low = prep_first(rhs, after(couple_prev, packed), diag_inverse)
    sent_even, moved_upper = hop(sent, within), hop(f0, within)
    f2, f3 = prep_second(couple_prev, g_high, g_low)
    moved_lower = hop(f2, within)
    halves = (f0, f1, f2, f3)
    base, sent = join(y, sent, sent_even, halves)
    moved = hop(sent, [(1, 3)])
    upper = pair_rows(moved_upper, halves)
    moved_lower = after(moved_lower, upper)
    pairs = (*upper, *pair_rows(moved_lower, halves))
    sent = advance(3, base, sent, moved, pairs)
    moved = hop(sent, [(3, 5)])
    near = jnp.stack([near[0]] + [after(part, sent) for part in near[1:]])
    parts = gather_far(near)
    moved = after(moved, near)
    sent = advance(5, base, sent, moved, pairs)
    moved, moved_even = hop(sent, [(5, 7)]), hop(sent, [(1, 2), (3, 4), (5, 6)])
    dense = clear()
    moved = after(moved, dense)
    sent = finish(base, sent, moved, moved_even, pairs, halves)
    parts = [parts[0]] + [after(part, sent) for part in parts[1:]]
    dense = build(owner_slot, parts, dense)
    line = gather_chips(sent, dense)
    other = swap_cores(line)
    update = products_other(dense, other, products_own(dense, line))
    return final(gather_far(jnp.stack(gather_near(update))), surface_factor, schur)


def solution(mesh):
    placed = (
        P("col", "row"),
        P("row", None),
        P("row", None),
        P(("row", "col"), None, None),
        P(("row", "col")),
        P(("row", "col")),
        P(("row", "col")),
        P("row", None),
        P("row", "col"),
        P(None, "col"),
    )
    return jax.shard_map(shards, mesh=mesh, in_specs=placed, out_specs=P("row", "col"), check_vma=False)
```

```python
import jax
import jax.numpy as jnp
from jax import lax
from jax.experimental import pallas as pl
from jax.experimental.pallas import tpu as pltpu
from jax.sharding import PartitionSpec as P

NB = 1024
BLK = 128
TILE = 16
TPD = 3
KCAP = 12
TPR = 48
SR = 768
NRHS = 512
N_ROW = 8
N_COL = 16
COLS = NRHS // N_COL
PER = NB // BLK
SIDE = 4
CHUNKS = 4
DIRECT = 2
BF = jnp.bfloat16
F32 = jnp.float32


def split(value):
    high = value.astype(BF)
    return high, (value - high.astype(F32)).astype(BF)


def in_hbm(value):
    return pltpu.with_memory_space_constraint(value, pltpu.HBM)


def mm(left, right):
    return jnp.dot(left, right, preferred_element_type=F32)


def vmem():
    return pl.BlockSpec(memory_space=pltpu.VMEM)


def smem():
    return pl.BlockSpec(memory_space=pltpu.SMEM)


def small(limit):
    return pltpu.CompilerParams(vmem_limit_bytes=limit << 20)


def hbm():
    return pl.BlockSpec(memory_space=pltpu.HBM)


def shape(rows, kind=BF):
    return jax.ShapeDtypeStruct((rows, NB), kind)


def with_split(left, high, low):
    first, second = split(left)
    both = mm(jnp.concatenate([first, second], axis=0), high)
    return both[: left.shape[0]] + both[left.shape[0] :] + mm(first, low)


def prep_body(rhs_hbm, e_hbm, g_hbm, sent_ref, y_ref, e_high, e_low, g_high, g_low, rhs_in, e_in, g_in, sems):
    rows = NB // CHUNKS
    moves = [pltpu.make_async_copy(rhs_hbm, rhs_in, sems.at[0])]
    for source, target in ((g_hbm, g_in), (e_hbm, e_in)):
        for at in range(CHUNKS):
            piece = pl.ds(at * rows, rows)
            moves.append(pltpu.make_async_copy(source.at[piece], target.at[piece], sems.at[len(moves)]))
    for move in moves:
        move.start()
    for at in range(CHUNKS):
        piece = pl.ds(at * rows, rows)
        moves[1 + at].wait()
        g_high[piece], g_low[piece] = split(g_in[piece])
    moves[0].wait()
    y = with_split(rhs_in[...], g_high[...], g_low[...])
    y_ref[...] = y
    sent_ref[...] = y.astype(BF)
    for at in range(CHUNKS):
        piece = pl.ds(at * rows, rows)
        moves[1 + CHUNKS + at].wait()
        e_high[piece], e_low[piece] = split(e_in[piece])


def prep(rhs, lower, inverse):
    return pl.pallas_call(
        prep_body,
        in_specs=[hbm()] * 3,
        out_specs=[vmem()] * 6,
        out_shape=[shape(COLS), shape(COLS, F32)] + [shape(NB)] * 4,
        scratch_shapes=[
            pltpu.VMEM((COLS, NB), F32),
            pltpu.VMEM((NB, NB), F32),
            pltpu.VMEM((NB, NB), F32),
            pltpu.SemaphoreType.DMA((1 + 2 * CHUNKS,)),
        ],
        compiler_params=small(12),
        name="prep",
    )(in_hbm(rhs), in_hbm(lower), in_hbm(inverse))


def change_body(e_high, e_low, g_high, g_low, high_ref, low_ref):
    rows = NB // CHUNKS

    @pl.when(lax.axis_index("row") > DIRECT)
    def _():
        for at in range(CHUNKS):
            piece = pl.ds(at * rows, rows)
            high, low = e_high[piece], e_low[piece]
            change = mm(high, g_high[...]) + mm(high, g_low[...]) + mm(low, g_high[...])
            high_ref[piece], low_ref[piece] = split(-change)


def change_of(factors):
    return pl.pallas_call(
        change_body,
        in_specs=[vmem()] * 4,
        out_specs=[vmem()] * 2,
        out_shape=[shape(NB)] * 2,
        compiler_params=small(10),
        name="change",
    )(*factors)


def advance(step, sent, before, start, factors):
    def body(sent_ref, start_ref, before_ref, *refs):
        *parts, out_ref = refs

        @pl.when(lax.axis_index("row") == step + 1)
        def _():
            moved = before_ref[...]
            product = mm(moved, parts[0][...]) + mm(moved, parts[1][...])
            if len(parts) == 4:
                x = with_split(start_ref[...] - product, parts[2][...], parts[3][...])
            else:
                x = start_ref[...] + product
            out_ref[...] = x.astype(BF)

    return pl.pallas_call(
        body,
        in_specs=[vmem()] * (3 + len(factors)),
        out_specs=vmem(),
        out_shape=shape(COLS),
        input_output_aliases={0: 0},
        compiler_params=small(4),
        name=f"advance{step}",
    )(sent, start, before, *factors)


def pack_body(blocks, tiles, count, slots, coupling_ref, out_ref, place):
    @pl.loop(0, TPR)
    def _(i):
        place[slots[0, i]] = i

    first = lax.axis_index("col") * TPD
    lane = lax.broadcasted_iota(jnp.int32, (TILE, BLK), 1)
    info = jnp.zeros((TILE, BLK), jnp.int32)
    values = []
    for k in range(KCAP):
        info = jnp.where(lane == k, blocks[k], info)
        info = jnp.where(lane == k + TILE, place[first + tiles[k]], info)
        tile = coupling_ref[k].astype(F32)
        values.append(jnp.where(k < count[0], tile, jnp.zeros_like(tile)))
        total = values[k]
        for before in range(k):
            same = (blocks[before] == blocks[k]) & (tiles[before] == tiles[k])
            total = total + jnp.where(same, values[before], jnp.zeros_like(tile))
        out_ref[k] = total.astype(BF)
    out_ref[KCAP] = info.astype(F32).astype(BF)


def pack(coupling, blocks, tiles, count, slots):
    return pl.pallas_call(
        pack_body,
        in_specs=[smem()] * 4 + [vmem()],
        out_specs=vmem(),
        out_shape=jax.ShapeDtypeStruct((KCAP + 1, TILE, BLK), BF),
        scratch_shapes=[pltpu.SMEM((TPR,), jnp.int32)],
        compiler_params=small(2),
        name="pack",
    )(blocks, tiles, count, slots, coupling)


def clear(earlier):
    def body(_, out_ref):
        out_ref[...] = jnp.zeros_like(out_ref)

    return pl.pallas_call(
        body,
        in_specs=[pl.BlockSpec(memory_space=pl.ANY)],
        out_specs=vmem(),
        out_shape=jax.ShapeDtypeStruct((N_ROW, SR, NB), BF),
        compiler_params=small(2),
        name="clear",
    )(earlier)


def build_body(cleared, c0, c1, c2, c3, out_ref, info, codes, sem):
    parts = (c0, c1, c2, c3)
    for part, ref in enumerate(parts):
        for z in range(SIDE):
            info[pl.ds(part * SIDE + z, 1)] = ref[z, KCAP].astype(F32)[:1].astype(jnp.int32)
    move = pltpu.make_async_copy(info, codes, sem)
    move.start()
    move.wait()
    for part, ref in enumerate(parts):

        @pl.loop(0, SIDE)
        def _(z):
            at = part * SIDE + z
            for k in range(KCAP):
                block = codes[at, k]
                row = pl.multiple_of(codes[at, k + TILE] * TILE, TILE)
                lane = pl.multiple_of(block % PER * BLK, BLK)
                out_ref[block // PER, pl.ds(row, TILE), pl.ds(lane, BLK)] = ref[z, k]


def build(parts, cleared):
    return pl.pallas_call(
        build_body,
        in_specs=[vmem()] * 5,
        out_specs=vmem(),
        input_output_aliases={0: 0},
        scratch_shapes=[
            pltpu.VMEM((N_COL, BLK), jnp.int32),
            pltpu.SMEM((N_COL, BLK), jnp.int32),
            pltpu.SemaphoreType.DMA(()),
        ],
        out_shape=jax.ShapeDtypeStruct((N_ROW, SR, NB), BF),
        compiler_params=small(4),
        name="build",
    )(cleared, *parts)


def line_sum(other, c_ref, x_ref):
    row = lax.axis_index("row")
    chip, core = row // 2, row % 2
    side = 1 - core if other else core
    total = None
    for k in range(SIDE):
        group = 2 * ((chip - k) % SIDE) + side
        part = lax.dot_general(c_ref[group], x_ref[k], (((1,), (1,)), ((), ())), preferred_element_type=F32)
        total = part if total is None else total + part
    return total


def own_body(c_ref, x_ref, out_ref):
    out_ref[...] = line_sum(False, c_ref, x_ref)


def other_body(c_ref, x_ref, sum_ref, out_ref):
    out_ref[...] = (sum_ref[...] + line_sum(True, c_ref, x_ref)).T.astype(BF)


def products_own(dense, line):
    return pl.pallas_call(
        own_body,
        in_specs=[vmem()] * 2,
        out_specs=vmem(),
        out_shape=jax.ShapeDtypeStruct((SR, COLS), F32),
        compiler_params=small(4),
        name="products_own",
    )(dense, line)


def products_other(dense, line, sums):
    return pl.pallas_call(
        other_body,
        in_specs=[vmem()] * 3,
        out_specs=vmem(),
        out_shape=jax.ShapeDtypeStruct((COLS, SR), BF),
        compiler_params=small(4),
        name="products_other",
    )(dense, line, sums)


def came_from(dx, dz):
    col = lax.axis_index("col")
    return (col // SIDE - dx) % SIDE * SIDE + (col % SIDE - dz) % SIDE


def final_body(*refs):
    pieces, (s_ref, schur_ref, out_hbm, stacked, turned, out, sems) = refs[:13], refs[13:]
    tall, wide, half = 256, 1024, COLS // 2

    def put(dx, dz, first, value):
        at = pl.multiple_of(came_from(dx, dz) * COLS + first, half)
        stacked[pl.ds(at, value.shape[0]), :] = value

    put(0, 0, 0, pieces[0][...])
    for k in range(1, SIDE):
        put(0, k, 0, pieces[k][...])
        put(k, 0, 0, pieces[3 + k][...])
        for other in range(1, SIDE):
            put(k, other, 0, pieces[6 + k][other - 1])
            put(other, k, half, pieces[9 + k][other - 1])
    moves = []
    for m in range(SR // tall):
        rows = pl.ds(m * tall, tall)
        turned[rows, :] = stacked[:, rows].T
        for n in range(schur_ref.shape[1] // wide):
            cols = pl.ds(n * wide, wide)
            slot = len(moves) % 4
            if len(moves) >= 4:
                moves[-4].wait()
            change = mm(turned[rows, :], s_ref[:, cols])
            out[slot] = (schur_ref[rows, cols].astype(F32) - change).astype(BF)
            moves.append(pltpu.make_async_copy(out.at[slot], out_hbm.at[rows, cols], sems.at[slot]))
            moves[-1].start()
    for move in moves[-4:]:
        move.wait()


def final(pieces, factor, schur):
    return pl.pallas_call(
        final_body,
        in_specs=[vmem()] * 15,
        out_specs=hbm(),
        scratch_shapes=[
            pltpu.VMEM((NRHS, SR), BF),
            pltpu.VMEM((SR, NRHS), BF),
            pltpu.VMEM((4, 256, 1024), BF),
            pltpu.SemaphoreType.DMA((4,)),
        ],
        out_shape=jax.ShapeDtypeStruct(schur.shape, BF),
        compiler_params=small(10),
        name="final",
    )(*pieces, factor, schur)


def turned_cols(value, dx, dz):
    pairs = [(x * SIDE + z, (x + dx) % SIDE * SIDE + (z + dz) % SIDE) for x in range(SIDE) for z in range(SIDE)]
    return lax.ppermute(value, "col", pairs)


def gather_near(value):
    return [value] + [turned_cols(value, 0, dz) for dz in (1, 2, 3)]


def gather_far(near):
    return [near] + [turned_cols(near, dx, 0) for dx in (1, 2, 3)]


def stack_halves(pieces, first):
    half = COLS // 2

    def body(a, b, c, out_ref):
        for at, ref in enumerate((a, b, c)):
            out_ref[at] = ref[first : first + half, :]

    return pl.pallas_call(
        body,
        in_specs=[vmem()] * 3,
        out_specs=vmem(),
        out_shape=jax.ShapeDtypeStruct((SIDE - 1, half, SR), BF),
        compiler_params=small(2),
        name=f"halves{first}",
    )(*pieces)


def gather_cols(value):
    half = COLS // 2
    along_z = [turned_cols(value, 0, k) for k in (1, 2, 3)]
    along_x = [turned_cols(value, k, 0) for k in (1, 2, 3)]
    first = stack_halves(along_z, 0)
    second = stack_halves(along_x, half)
    others = [turned_cols(first, k, 0) for k in (1, 2, 3)] + [turned_cols(second, 0, k) for k in (1, 2, 3)]
    return [value] + along_z + along_x + others


def gather_chips(value, first):
    def moved(k):
        return lax.ppermute(value, "row", [(2 * a + c, 2 * ((a + k) % SIDE) + c) for a in range(SIDE) for c in (0, 1)])

    return jnp.stack([value] + [after(moved(k), first) for k in (1, 2, 3)])


def swap_cores(value):
    return lax.ppermute(value, "row", [(i, i ^ 1) for i in range(N_ROW)])


def after(value, earlier):
    return lax.optimization_barrier((value, earlier))[0]


def shards(rhs, couple_prev, diag_inverse, coupling, pair_block, pair_tile, pair_count, owner_slot, schur, surface_factor):
    sent, y, e_high, e_low, g_high, g_low = prep(rhs, couple_prev, diag_inverse)
    factors = (e_high, e_low, g_high, g_low)
    change = near = parts = cleared = None
    for step in range(N_ROW - 1):
        before = lax.ppermute(sent, "row", [(step, step + 1)])
        if step == DIRECT:
            change = change_of((after(e_high, sent), *factors[1:]))
            before = after(before, change)
        if step == 3:
            near = gather_near(pack(after(coupling, sent), pair_block, pair_tile, pair_count, owner_slot))
        if step == 4:
            near = jnp.stack([near[0]] + [after(part, sent) for part in near[1:]])
            parts = gather_far(near)
            before = after(before, near)
        if step == 5:
            cleared = clear(sent)
            before = after(before, cleared)
        if step < DIRECT:
            sent = advance(step, sent, before, rhs, factors)
        else:
            sent = advance(step, sent, before, y, change)
    dense = build([parts[0]] + [after(part, sent) for part in parts[1:]], cleared)
    line = gather_chips(sent, dense)
    other = swap_cores(line)
    update = products_other(dense, other, products_own(dense, line))
    return final(gather_cols(update), surface_factor, schur)


def solution(mesh):
    placed = (
        P("col", "row"),
        P("row", None),
        P("row", None),
        P(("row", "col"), None, None),
        P(("row", "col")),
        P(("row", "col")),
        P(("row", "col")),
        P("row", None),
        P("row", "col"),
        P(None, "col"),
    )
    return jax.shard_map(shards, mesh=mesh, in_specs=placed, out_specs=P("row", "col"), check_vma=False)
```

```python
import jax
import jax.numpy as jnp
from jax import lax
from jax.experimental import pallas as pl
from jax.experimental.pallas import tpu as pltpu
from jax.sharding import PartitionSpec as P

NB = 1024
BLK = 128
TILE = 16
TPD = 3
KCAP = 12
TPR = 48
SR = 768
NRHS = 512
N_ROW = 8
N_COL = 16
COLS = NRHS // N_COL
PER = NB // BLK
SIDE = 4
CHUNKS = 4
BF = jnp.bfloat16
F32 = jnp.float32


def split(value):
    high = value.astype(BF)
    return high, (value - high.astype(F32)).astype(BF)


def in_hbm(value):
    return pltpu.with_memory_space_constraint(value, pltpu.HBM)


def mm(left, right):
    return jnp.dot(left, right, preferred_element_type=F32)


def vmem():
    return pl.BlockSpec(memory_space=pltpu.VMEM)


def smem():
    return pl.BlockSpec(memory_space=pltpu.SMEM)


def small(limit):
    return pltpu.CompilerParams(vmem_limit_bytes=limit << 20)


def hbm():
    return pl.BlockSpec(memory_space=pltpu.HBM)


def shape(rows, kind=BF):
    return jax.ShapeDtypeStruct((rows, NB), kind)


def with_split(left, high, low):
    first, second = split(left)
    both = mm(jnp.concatenate([first, second], axis=0), high)
    return both[: left.shape[0]] + both[left.shape[0] :] + mm(first, low)


def prep_body(rhs_hbm, e_hbm, g_hbm, sent_ref, e_high, e_low, g_high, g_low, rhs_in, e_in, g_in, sems):
    rows = NB // CHUNKS
    moves = [pltpu.make_async_copy(rhs_hbm, rhs_in, sems.at[0])]
    for source, target in ((g_hbm, g_in), (e_hbm, e_in)):
        for at in range(CHUNKS):
            piece = pl.ds(at * rows, rows)
            moves.append(pltpu.make_async_copy(source.at[piece], target.at[piece], sems.at[len(moves)]))
    for move in moves:
        move.start()
    for at in range(CHUNKS):
        piece = pl.ds(at * rows, rows)
        moves[1 + at].wait()
        g_high[piece], g_low[piece] = split(g_in[piece])
    moves[0].wait()
    sent_ref[...] = with_split(rhs_in[...], g_high[...], g_low[...]).astype(BF)
    for at in range(CHUNKS):
        piece = pl.ds(at * rows, rows)
        moves[1 + CHUNKS + at].wait()
        e_high[piece], e_low[piece] = split(e_in[piece])


def prep(rhs, lower, inverse):
    return pl.pallas_call(
        prep_body,
        in_specs=[hbm()] * 3,
        out_specs=[vmem()] * 5,
        out_shape=[shape(COLS)] + [shape(NB)] * 4,
        scratch_shapes=[
            pltpu.VMEM((COLS, NB), F32),
            pltpu.VMEM((NB, NB), F32),
            pltpu.VMEM((NB, NB), F32),
            pltpu.SemaphoreType.DMA((1 + 2 * CHUNKS,)),
        ],
        compiler_params=small(12),
        name="prep",
    )(in_hbm(rhs), in_hbm(lower), in_hbm(inverse))


def advance(step, sent, before, rhs, factors):
    def body(sent_ref, rhs_ref, before_ref, e_high, e_low, g_high, g_low, out_ref):
        @pl.when(lax.axis_index("row") == step + 1)
        def _():
            moved = before_ref[...]
            right = rhs_ref[...] - mm(moved, e_high[...]) - mm(moved, e_low[...])
            out_ref[...] = with_split(right, g_high[...], g_low[...]).astype(BF)

    return pl.pallas_call(
        body,
        in_specs=[vmem()] * 7,
        out_specs=vmem(),
        out_shape=shape(COLS),
        input_output_aliases={0: 0},
        compiler_params=small(4),
    )(sent, rhs, before, *factors)


def pack_body(blocks, tiles, count, slots, coupling_ref, out_ref, place):
    @pl.loop(0, TPR)
    def _(i):
        place[slots[0, i]] = i

    first = lax.axis_index("col") * TPD
    lane = lax.broadcasted_iota(jnp.int32, (TILE, BLK), 1)
    info = jnp.zeros((TILE, BLK), jnp.int32)
    values = []
    for k in range(KCAP):
        info = jnp.where(lane == k, blocks[k], info)
        info = jnp.where(lane == k + TILE, place[first + tiles[k]], info)
        tile = coupling_ref[k].astype(F32)
        values.append(jnp.where(k < count[0], tile, jnp.zeros_like(tile)))
        total = values[k]
        for before in range(k):
            same = (blocks[before] == blocks[k]) & (tiles[before] == tiles[k])
            total = total + jnp.where(same, values[before], jnp.zeros_like(tile))
        out_ref[k] = total.astype(BF)
    out_ref[KCAP] = info.astype(F32).astype(BF)


def pack(coupling, blocks, tiles, count, slots):
    return pl.pallas_call(
        pack_body,
        in_specs=[smem()] * 4 + [vmem()],
        out_specs=vmem(),
        out_shape=jax.ShapeDtypeStruct((KCAP + 1, TILE, BLK), BF),
        scratch_shapes=[pltpu.SMEM((TPR,), jnp.int32)],
        compiler_params=small(2),
        name="pack",
    )(blocks, tiles, count, slots, coupling)


def clear(earlier):
    def body(_, out_ref):
        out_ref[...] = jnp.zeros_like(out_ref)

    return pl.pallas_call(
        body,
        in_specs=[pl.BlockSpec(memory_space=pl.ANY)],
        out_specs=vmem(),
        out_shape=jax.ShapeDtypeStruct((N_ROW, SR, NB), BF),
        compiler_params=small(2),
        name="clear",
    )(earlier)


def build_body(cleared, c0, c1, c2, c3, out_ref, info, codes, sem):
    parts = (c0, c1, c2, c3)
    for part, ref in enumerate(parts):
        for z in range(SIDE):
            info[pl.ds(part * SIDE + z, 1)] = ref[z, KCAP].astype(F32)[:1].astype(jnp.int32)
    move = pltpu.make_async_copy(info, codes, sem)
    move.start()
    move.wait()
    for part, ref in enumerate(parts):

        @pl.loop(0, SIDE)
        def _(z):
            at = part * SIDE + z
            for k in range(KCAP):
                block = codes[at, k]
                row = pl.multiple_of(codes[at, k + TILE] * TILE, TILE)
                lane = pl.multiple_of(block % PER * BLK, BLK)
                out_ref[block // PER, pl.ds(row, TILE), pl.ds(lane, BLK)] = ref[z, k]


def build(parts, cleared):
    return pl.pallas_call(
        build_body,
        in_specs=[vmem()] * 5,
        out_specs=vmem(),
        input_output_aliases={0: 0},
        scratch_shapes=[
            pltpu.VMEM((N_COL, BLK), jnp.int32),
            pltpu.SMEM((N_COL, BLK), jnp.int32),
            pltpu.SemaphoreType.DMA(()),
        ],
        out_shape=jax.ShapeDtypeStruct((N_ROW, SR, NB), BF),
        compiler_params=small(4),
        name="build",
    )(cleared, *parts)


def line_sum(other, c_ref, x_ref):
    row = lax.axis_index("row")
    chip, core = row // 2, row % 2
    side = 1 - core if other else core
    total = None
    for k in range(SIDE):
        group = 2 * ((chip - k) % SIDE) + side
        part = lax.dot_general(c_ref[group], x_ref[k], (((1,), (1,)), ((), ())), preferred_element_type=F32)
        total = part if total is None else total + part
    return total


def own_body(c_ref, x_ref, out_ref):
    out_ref[...] = line_sum(False, c_ref, x_ref)


def other_body(c_ref, x_ref, sum_ref, out_ref):
    out_ref[...] = (sum_ref[...] + line_sum(True, c_ref, x_ref)).T.astype(BF)


def products_own(dense, line):
    return pl.pallas_call(
        own_body,
        in_specs=[vmem()] * 2,
        out_specs=vmem(),
        out_shape=jax.ShapeDtypeStruct((SR, COLS), F32),
        compiler_params=small(4),
        name="products_own",
    )(dense, line)


def products_other(dense, line, sums):
    return pl.pallas_call(
        other_body,
        in_specs=[vmem()] * 3,
        out_specs=vmem(),
        out_shape=jax.ShapeDtypeStruct((COLS, SR), BF),
        compiler_params=small(4),
        name="products_other",
    )(dense, line, sums)


def came_from(dx, dz):
    col = lax.axis_index("col")
    return (col // SIDE - dx) % SIDE * SIDE + (col % SIDE - dz) % SIDE


def final_body(*refs):
    pieces, (s_ref, schur_ref, out_hbm, stacked, turned, out, sems) = refs[:13], refs[13:]
    tall, wide, half = 256, 1024, COLS // 2

    def put(dx, dz, first, value):
        at = pl.multiple_of(came_from(dx, dz) * COLS + first, half)
        stacked[pl.ds(at, value.shape[0]), :] = value

    put(0, 0, 0, pieces[0][...])
    for k in range(1, SIDE):
        put(0, k, 0, pieces[k][...])
        put(k, 0, 0, pieces[3 + k][...])
        for other in range(1, SIDE):
            put(k, other, 0, pieces[6 + k][other - 1])
            put(other, k, half, pieces[9 + k][other - 1])
    moves = []
    for m in range(SR // tall):
        rows = pl.ds(m * tall, tall)
        turned[rows, :] = stacked[:, rows].T
        for n in range(schur_ref.shape[1] // wide):
            cols = pl.ds(n * wide, wide)
            slot = len(moves) % 4
            if len(moves) >= 4:
                moves[-4].wait()
            change = mm(turned[rows, :], s_ref[:, cols])
            out[slot] = (schur_ref[rows, cols].astype(F32) - change).astype(BF)
            moves.append(pltpu.make_async_copy(out.at[slot], out_hbm.at[rows, cols], sems.at[slot]))
            moves[-1].start()
    for move in moves[-4:]:
        move.wait()


def final(pieces, factor, schur):
    return pl.pallas_call(
        final_body,
        in_specs=[vmem()] * 15,
        out_specs=hbm(),
        scratch_shapes=[
            pltpu.VMEM((NRHS, SR), BF),
            pltpu.VMEM((SR, NRHS), BF),
            pltpu.VMEM((4, 256, 1024), BF),
            pltpu.SemaphoreType.DMA((4,)),
        ],
        out_shape=jax.ShapeDtypeStruct(schur.shape, BF),
        compiler_params=small(10),
        name="final",
    )(*pieces, factor, schur)


def turned_cols(value, dx, dz):
    pairs = [(x * SIDE + z, (x + dx) % SIDE * SIDE + (z + dz) % SIDE) for x in range(SIDE) for z in range(SIDE)]
    return lax.ppermute(value, "col", pairs)


def gather_near(value):
    return [value] + [turned_cols(value, 0, dz) for dz in (1, 2, 3)]


def gather_far(near):
    return [near] + [turned_cols(near, dx, 0) for dx in (1, 2, 3)]


def stack_halves(pieces, first):
    half = COLS // 2

    def body(a, b, c, out_ref):
        for at, ref in enumerate((a, b, c)):
            out_ref[at] = ref[first : first + half, :]

    return pl.pallas_call(
        body,
        in_specs=[vmem()] * 3,
        out_specs=vmem(),
        out_shape=jax.ShapeDtypeStruct((SIDE - 1, half, SR), BF),
        compiler_params=small(2),
    )(*pieces)


def gather_cols(value):
    half = COLS // 2
    along_z = [turned_cols(value, 0, k) for k in (1, 2, 3)]
    along_x = [turned_cols(value, k, 0) for k in (1, 2, 3)]
    first = stack_halves(along_z, 0)
    second = stack_halves(along_x, half)
    others = [turned_cols(first, k, 0) for k in (1, 2, 3)] + [turned_cols(second, 0, k) for k in (1, 2, 3)]
    return [value] + along_z + along_x + others


def gather_chips(value, first):
    def moved(k):
        return lax.ppermute(value, "row", [(2 * a + c, 2 * ((a + k) % SIDE) + c) for a in range(SIDE) for c in (0, 1)])

    return jnp.stack([value] + [after(moved(k), first) for k in (1, 2, 3)])


def swap_cores(value):
    return lax.ppermute(value, "row", [(i, i ^ 1) for i in range(N_ROW)])


def after(value, earlier):
    return lax.optimization_barrier((value, earlier))[0]


def shards(rhs, couple_prev, diag_inverse, coupling, pair_block, pair_tile, pair_count, owner_slot, schur, surface_factor):
    sent, *factors = prep(rhs, couple_prev, diag_inverse)
    near = parts = packed = cleared = None
    for step in range(N_ROW - 1):
        before = lax.ppermute(sent, "row", [(step, step + 1)])
        if step == 1:
            packed = pack(after(coupling, sent), pair_block, pair_tile, pair_count, owner_slot)
            before = after(before, packed)
        if step == 2:
            near = gather_near(packed)
        if step == 3:
            before = after(before, near)
        if step == 4:
            near = jnp.stack([near[0]] + [after(part, sent) for part in near[1:]])
            parts = gather_far(near)
            before = after(before, near)
        if step == 5:
            cleared = clear(sent)
            before = after(before, cleared)
        sent = advance(step, sent, before, rhs, factors)
    dense = build([parts[0]] + [after(part, sent) for part in parts[1:]], cleared)
    line = gather_chips(sent, dense)
    other = swap_cores(line)
    update = products_other(dense, other, products_own(dense, line))
    return final(gather_cols(update), surface_factor, schur)


def solution(mesh):
    placed = (
        P("col", "row"),
        P("row", None),
        P("row", None),
        P(("row", "col"), None, None),
        P(("row", "col")),
        P(("row", "col")),
        P(("row", "col")),
        P("row", None),
        P("row", "col"),
        P(None, "col"),
    )

    return jax.shard_map(shards, mesh=mesh, in_specs=placed, out_specs=P("row", "col"), check_vma=False)
```

```python
import jax
import jax.numpy as jnp
from jax import lax
from jax.experimental import pallas as pl
from jax.experimental.pallas import tpu as pltpu
from jax.sharding import PartitionSpec as P

NB = 1024
BLK = 128
TILE = 16
TPD = 3
KCAP = 12
TPR = 48
SR = 768
NRHS = 512
N_ROW = 8
N_COL = 16
COLS = NRHS // N_COL
PER = NB // BLK
SIDE = 4
CHUNKS = 4
WIDE = 512
BF = jnp.bfloat16
F32 = jnp.float32


def split(value):
    high = value.astype(BF)
    return high, (value - high.astype(F32)).astype(BF)


def in_hbm(value):
    return pltpu.with_memory_space_constraint(value, pltpu.HBM)


def mm(left, right):
    return jnp.dot(left, right, preferred_element_type=F32)


def vmem():
    return pl.BlockSpec(memory_space=pltpu.VMEM)


def smem():
    return pl.BlockSpec(memory_space=pltpu.SMEM)


def small(limit):
    return pltpu.CompilerParams(vmem_limit_bytes=limit << 20)


def hbm():
    return pl.BlockSpec(memory_space=pltpu.HBM)


def shape(rows, kind=BF):
    return jax.ShapeDtypeStruct((rows, NB), kind)


def with_split(left, high, low):
    first, second = split(left)
    both = mm(jnp.concatenate([first, second], axis=0), high)
    return both[: left.shape[0]] + both[left.shape[0] :] + mm(first, low)


def prep_body(rhs_hbm, e_hbm, g_hbm, sent_ref, e_high, e_low, g_high, g_low, rhs_in, e_in, g_in, sems):
    rows = NB // CHUNKS
    moves = [pltpu.make_async_copy(rhs_hbm, rhs_in, sems.at[0])]
    for source, target in ((g_hbm, g_in), (e_hbm, e_in)):
        for at in range(CHUNKS):
            piece = pl.ds(at * rows, rows)
            moves.append(pltpu.make_async_copy(source.at[piece], target.at[piece], sems.at[len(moves)]))
    for move in moves:
        move.start()
    for at in range(CHUNKS):
        piece = pl.ds(at * rows, rows)
        moves[1 + at].wait()
        g_high[piece], g_low[piece] = split(g_in[piece])
    moves[0].wait()
    sent_ref[...] = with_split(rhs_in[...], g_high[...], g_low[...]).astype(BF)
    for at in range(CHUNKS):
        piece = pl.ds(at * rows, rows)
        moves[1 + CHUNKS + at].wait()
        e_high[piece], e_low[piece] = split(e_in[piece])


def prep(rhs, lower, inverse):
    return pl.pallas_call(
        prep_body,
        in_specs=[hbm()] * 3,
        out_specs=[vmem()] * 5,
        out_shape=[shape(COLS)] + [shape(NB)] * 4,
        scratch_shapes=[
            pltpu.VMEM((COLS, NB), F32),
            pltpu.VMEM((NB, NB), F32),
            pltpu.VMEM((NB, NB), F32),
            pltpu.SemaphoreType.DMA((1 + 2 * CHUNKS,)),
        ],
        compiler_params=small(12),
        name="prep",
    )(in_hbm(rhs), in_hbm(lower), in_hbm(inverse))


def advance(step, sent, before, rhs, factors):
    def body(sent_ref, rhs_ref, before_ref, e_high, e_low, g_high, g_low, out_ref):
        @pl.when(lax.axis_index("row") == step + 1)
        def _():
            moved = before_ref[...]
            right = rhs_ref[...] - mm(moved, e_high[...]) - mm(moved, e_low[...])
            out_ref[...] = with_split(right, g_high[...], g_low[...]).astype(BF)

    return pl.pallas_call(
        body,
        in_specs=[vmem()] * 7,
        out_specs=vmem(),
        out_shape=shape(COLS),
        input_output_aliases={0: 0},
        compiler_params=small(4),
    )(sent, rhs, before, *factors)


def pack_body(blocks, tiles, count, slots, coupling_ref, out_ref, place):
    @pl.loop(0, TPR)
    def _(i):
        place[slots[0, i]] = i

    first = lax.axis_index("col") * TPD
    lane = lax.broadcasted_iota(jnp.int32, (TILE, BLK), 1)
    info = jnp.zeros((TILE, BLK), jnp.int32)
    values = []
    for k in range(KCAP):
        info = jnp.where(lane == k, blocks[k], info)
        info = jnp.where(lane == k + TILE, place[first + tiles[k]], info)
        tile = coupling_ref[k].astype(F32)
        values.append(jnp.where(k < count[0], tile, jnp.zeros_like(tile)))
        total = values[k]
        for before in range(k):
            same = (blocks[before] == blocks[k]) & (tiles[before] == tiles[k])
            total = total + jnp.where(same, values[before], jnp.zeros_like(tile))
        out_ref[k] = total.astype(BF)
    out_ref[KCAP] = info.astype(F32).astype(BF)


def pack(coupling, blocks, tiles, count, slots):
    return pl.pallas_call(
        pack_body,
        in_specs=[smem()] * 4 + [vmem()],
        out_specs=vmem(),
        out_shape=jax.ShapeDtypeStruct((KCAP + 1, TILE, BLK), BF),
        scratch_shapes=[pltpu.SMEM((TPR,), jnp.int32)],
        compiler_params=small(2),
        name="pack",
    )(blocks, tiles, count, slots, coupling)


def clear(earlier):
    def body(_, out_ref):
        out_ref[...] = jnp.zeros_like(out_ref)

    return pl.pallas_call(
        body,
        in_specs=[pl.BlockSpec(memory_space=pl.ANY)],
        out_specs=vmem(),
        out_shape=jax.ShapeDtypeStruct((N_ROW, SR, NB), BF),
        compiler_params=small(2),
        name="clear",
    )(earlier)


def build_body(cleared, c0, c1, c2, c3, out_ref, info, codes, sem):
    parts = (c0, c1, c2, c3)
    for part, ref in enumerate(parts):
        for z in range(SIDE):
            info[pl.ds(part * SIDE + z, 1)] = ref[z, KCAP].astype(F32)[:1].astype(jnp.int32)
    move = pltpu.make_async_copy(info, codes, sem)
    move.start()
    move.wait()
    for part, ref in enumerate(parts):

        @pl.loop(0, SIDE)
        def _(z):
            at = part * SIDE + z
            for k in range(KCAP):
                block = codes[at, k]
                row = pl.multiple_of(codes[at, k + TILE] * TILE, TILE)
                lane = pl.multiple_of(block % PER * BLK, BLK)
                out_ref[block // PER, pl.ds(row, TILE), pl.ds(lane, BLK)] = ref[z, k]


def build(parts, cleared):
    return pl.pallas_call(
        build_body,
        in_specs=[vmem()] * 5,
        out_specs=vmem(),
        input_output_aliases={0: 0},
        scratch_shapes=[
            pltpu.VMEM((N_COL, BLK), jnp.int32),
            pltpu.SMEM((N_COL, BLK), jnp.int32),
            pltpu.SemaphoreType.DMA(()),
        ],
        out_shape=jax.ShapeDtypeStruct((N_ROW, SR, NB), BF),
        compiler_params=small(4),
        name="build",
    )(cleared, *parts)


def line_sum(other, c_ref, x_ref):
    row = lax.axis_index("row")
    chip, core = row // 2, row % 2
    side = 1 - core if other else core
    total = None
    for k in range(SIDE):
        group = 2 * ((chip - k) % SIDE) + side
        part = lax.dot_general(c_ref[group], x_ref[k], (((1,), (1,)), ((), ())), preferred_element_type=F32)
        total = part if total is None else total + part
    return total


def own_body(c_ref, x_ref, out_ref):
    out_ref[...] = line_sum(False, c_ref, x_ref)


def other_body(c_ref, x_ref, sum_ref, out_ref):
    out_ref[...] = (sum_ref[...] + line_sum(True, c_ref, x_ref)).T.astype(BF)


def products_own(dense, line):
    return pl.pallas_call(
        own_body,
        in_specs=[vmem()] * 2,
        out_specs=vmem(),
        out_shape=jax.ShapeDtypeStruct((SR, COLS), F32),
        compiler_params=small(4),
        name="products_own",
    )(dense, line)


def products_other(dense, line, sums):
    return pl.pallas_call(
        other_body,
        in_specs=[vmem()] * 3,
        out_specs=vmem(),
        out_shape=jax.ShapeDtypeStruct((COLS, SR), BF),
        compiler_params=small(4),
        name="products_other",
    )(dense, line, sums)


def change_blocks(parts, shifts, s_ref, stacked, turned):
    col = lax.axis_index("col")
    span = SIDE * COLS
    bases = []
    for at, (ref, dx) in enumerate(zip(parts, shifts)):
        for dz in range(SIDE):
            spot = pl.multiple_of(at * span + (col % SIDE - dz) % SIDE * COLS, COLS)
            stacked[pl.ds(spot, COLS), :] = ref[dz]
        bases.append(pl.ds(pl.multiple_of((col // SIDE - dx) % SIDE * span, span), span))
    turned[...] = stacked[...].T
    for n in range(s_ref.shape[1] // WIDE):
        cols = pl.ds(n * WIDE, WIDE)
        factor = jnp.concatenate([s_ref[base, cols] for base in bases], axis=0)
        yield n, cols, mm(turned[...], factor)


def half_scratch():
    return [pltpu.VMEM((2 * SIDE * COLS, SR), BF), pltpu.VMEM((SR, 2 * SIDE * COLS), BF)]


def final_first(near, far, factor, schur):
    def body(w0, w1, s_ref, schur_ref, out_ref, stacked, turned):
        for _, cols, change in change_blocks((w0, w1), (0, 1), s_ref, stacked, turned):
            out_ref[:, cols] = schur_ref[:, cols].astype(F32) - change

    return pl.pallas_call(
        body,
        in_specs=[vmem()] * 4,
        out_specs=vmem(),
        scratch_shapes=half_scratch(),
        out_shape=jax.ShapeDtypeStruct(schur.shape, F32),
        compiler_params=small(8),
        name="final_first",
    )(near, far, factor, schur)


def final_second(parts, factor, partial):
    def body(w2, w3, s_ref, part_ref, out_hbm, stacked, turned, out, sems):
        moves = []
        for n, cols, change in change_blocks((w2, w3), (2, 3), s_ref, stacked, turned):
            slot = n % SIDE
            if n >= SIDE:
                moves[-SIDE].wait()
            out[slot] = (part_ref[:, cols] - change).astype(BF)
            moves.append(pltpu.make_async_copy(out.at[slot], out_hbm.at[:, cols], sems.at[slot]))
            moves[-1].start()
        for move in moves[-SIDE:]:
            move.wait()

    return pl.pallas_call(
        body,
        in_specs=[vmem()] * 4,
        out_specs=hbm(),
        scratch_shapes=half_scratch() + [pltpu.VMEM((SIDE, SR, WIDE), BF), pltpu.SemaphoreType.DMA((SIDE,))],
        out_shape=jax.ShapeDtypeStruct(partial.shape, BF),
        compiler_params=small(12),
        name="final_second",
    )(*parts, factor, partial)


def turned_cols(value, dx, dz):
    pairs = [(x * SIDE + z, (x + dx) % SIDE * SIDE + (z + dz) % SIDE) for x in range(SIDE) for z in range(SIDE)]
    return lax.ppermute(value, "col", pairs)


def gather_near(value):
    return [value] + [turned_cols(value, 0, dz) for dz in (1, 2, 3)]


def gather_far(near):
    return [near] + [turned_cols(near, dx, 0) for dx in (1, 2, 3)]


def gather_chips(value, first):
    def moved(k):
        return lax.ppermute(value, "row", [(2 * a + c, 2 * ((a + k) % SIDE) + c) for a in range(SIDE) for c in (0, 1)])

    return jnp.stack([value] + [after(moved(k), first) for k in (1, 2, 3)])


def swap_cores(value):
    return lax.ppermute(value, "row", [(i, i ^ 1) for i in range(N_ROW)])


def after(value, earlier):
    return lax.optimization_barrier((value, earlier))[0]


def shards(rhs, couple_prev, diag_inverse, coupling, pair_block, pair_tile, pair_count, owner_slot, schur, surface_factor):
    sent, *factors = prep(rhs, couple_prev, diag_inverse)
    near = parts = packed = cleared = None
    for step in range(N_ROW - 1):
        before = lax.ppermute(sent, "row", [(step, step + 1)])
        if step == 1:
            packed = pack(after(coupling, sent), pair_block, pair_tile, pair_count, owner_slot)
            before = after(before, packed)
        if step == 2:
            near = gather_near(packed)
        if step == 3:
            before = after(before, near)
        if step == 4:
            near = jnp.stack([near[0]] + [after(part, sent) for part in near[1:]])
            parts = gather_far(near)
            before = after(before, near)
        if step == 5:
            cleared = clear(sent)
            before = after(before, cleared)
        sent = advance(step, sent, before, rhs, factors)
    dense = build([parts[0]] + [after(part, sent) for part in parts[1:]], cleared)
    line = gather_chips(sent, dense)
    other = swap_cores(line)
    update = products_other(dense, other, products_own(dense, line))
    pieces = [update]
    for k in (1, 2, 3):
        pieces.append(turned_cols(update, 0, k))
    near = jnp.stack(pieces)
    far = []
    for k in (1, 2, 3):
        far.append(turned_cols(near, k, 0))
    partial = final_first(near, far[0], surface_factor, schur)
    return final_second([after(part, partial) for part in far[1:]], surface_factor, partial)


def solution(mesh):
    placed = (
        P("col", "row"),
        P("row", None),
        P("row", None),
        P(("row", "col"), None, None),
        P(("row", "col")),
        P(("row", "col")),
        P(("row", "col")),
        P("row", None),
        P("row", "col"),
        P(None, "col"),
    )

    return jax.shard_map(shards, mesh=mesh, in_specs=placed, out_specs=P("row", "col"), check_vma=False)
```

```python
import jax
import jax.numpy as jnp
from jax import lax
from jax.experimental import pallas as pl
from jax.experimental.pallas import tpu as pltpu
from jax.sharding import PartitionSpec as P

NB = 1024
BLK = 128
TILE = 16
TPD = 3
KCAP = 12
TPR = 48
SR = 768
NRHS = 512
N_ROW = 8
N_COL = 16
COLS = NRHS // N_COL
PER = NB // BLK
SIDE = 4
CHUNKS = 4
WIDE = 512
BF = jnp.bfloat16
F32 = jnp.float32


def split(value):
    high = value.astype(BF)
    return high, (value - high.astype(F32)).astype(BF)


def in_hbm(value):
    return pltpu.with_memory_space_constraint(value, pltpu.HBM)


def mm(left, right):
    return jnp.dot(left, right, preferred_element_type=F32)


def vmem():
    return pl.BlockSpec(memory_space=pltpu.VMEM)


def smem():
    return pl.BlockSpec(memory_space=pltpu.SMEM)


def small(limit):
    return pltpu.CompilerParams(vmem_limit_bytes=limit << 20)


def hbm():
    return pl.BlockSpec(memory_space=pltpu.HBM)


def shape(rows, kind=BF):
    return jax.ShapeDtypeStruct((rows, NB), kind)


def with_split(left, high, low):
    first, second = split(left)
    both = mm(jnp.concatenate([first, second], axis=0), high)
    return both[: left.shape[0]] + both[left.shape[0] :] + mm(first, low)


def loads(source, target, sems, first, skip):
    rows = NB // CHUNKS
    moves = []
    for at in range(target.shape[0] // rows):
        piece = source.at[pl.ds(skip + at * rows, rows)]
        moves.append(pltpu.make_async_copy(piece, target.at[pl.ds(at * rows, rows)], sems.at[first + at]))
        moves[-1].start()
    return moves


def split_arriving(moves, source, high_ref, low_ref):
    rows = NB // CHUNKS
    for at, move in enumerate(moves):
        piece = pl.ds(at * rows, rows)
        move.wait()
        high_ref[piece], low_ref[piece] = split(source[piece])


def first_body(rhs_hbm, e_hbm, g_hbm, sent_ref, g_high, g_low, e_high, e_low, rhs_in, e_in, g_in, sems):
    fetch = pltpu.make_async_copy(rhs_hbm, rhs_in, sems.at[0])
    fetch.start()
    g_moves = loads(g_hbm, g_in, sems, 1, 0)
    e_moves = loads(e_hbm, e_in, sems, 1 + CHUNKS, 0)
    split_arriving(g_moves, g_in, g_high, g_low)
    fetch.wait()
    sent_ref[...] = with_split(rhs_in[...], g_high[...], g_low[...]).astype(BF)
    split_arriving(e_moves, e_in, e_high, e_low)


def second_body(e_hbm, _, e_high, e_low, e_in, sems):
    split_arriving(loads(e_hbm, e_in, sems, 0, NB // 2), e_in, e_high, e_low)


def prep_first(rhs, lower, inverse):
    half = NB // 2
    return pl.pallas_call(
        first_body,
        in_specs=[hbm()] * 3,
        out_specs=[vmem()] * 5,
        out_shape=[shape(COLS), shape(NB), shape(NB), shape(half), shape(half)],
        scratch_shapes=[
            pltpu.VMEM((COLS, NB), F32),
            pltpu.VMEM((half, NB), F32),
            pltpu.VMEM((NB, NB), F32),
            pltpu.SemaphoreType.DMA((1 + 2 * CHUNKS,)),
        ],
        compiler_params=small(12),
        name="prep_first",
    )(in_hbm(rhs), in_hbm(lower), in_hbm(inverse))


def prep_second(lower, earlier):
    half = NB // 2
    return pl.pallas_call(
        second_body,
        in_specs=[hbm(), pl.BlockSpec(memory_space=pl.ANY)],
        out_specs=[vmem()] * 2,
        out_shape=[shape(half)] * 2,
        scratch_shapes=[pltpu.VMEM((half, NB), F32), pltpu.SemaphoreType.DMA((CHUNKS,))],
        compiler_params=small(8),
        name="prep_second",
    )(in_hbm(lower), earlier)


def change_body(rhs_ref, g_high, g_low, e0, e1, e2, e3, y_ref, high_ref, low_ref):
    rows, half = NB // CHUNKS, NB // 2

    @pl.when(lax.axis_index("row") == N_ROW - 1)
    def _():
        y_ref[...] = with_split(rhs_ref[...], g_high[...], g_low[...])
        for at in range(CHUNKS):
            high_e, low_e = (e0, e1) if at * rows < half else (e2, e3)
            piece = pl.ds(at * rows % half, rows)
            high, low = high_e[piece], low_e[piece]
            change = mm(high, g_high[...]) + mm(high, g_low[...]) + mm(low, g_high[...])
            high_ref[pl.ds(at * rows, rows)], low_ref[pl.ds(at * rows, rows)] = split(-change)


def change_of(rhs, factors):
    return pl.pallas_call(
        change_body,
        in_specs=[vmem()] * 7,
        out_specs=[vmem()] * 3,
        out_shape=[shape(COLS, F32), shape(NB), shape(NB)],
        compiler_params=small(10),
        name="change",
    )(rhs, *factors)


def advance(step, sent, before, rhs, factors):
    def body(sent_ref, rhs_ref, before_ref, g_high, g_low, e0, e1, e2, e3, out_ref):
        half = NB // 2

        @pl.when(lax.axis_index("row") == step + 1)
        def _():
            upper, lower = before_ref[:, :half], before_ref[:, half:]
            right = rhs_ref[...] - mm(upper, e0[...]) - mm(upper, e1[...]) - mm(lower, e2[...]) - mm(lower, e3[...])
            out_ref[...] = with_split(right, g_high[...], g_low[...]).astype(BF)

    return pl.pallas_call(
        body,
        in_specs=[vmem()] * 9,
        out_specs=vmem(),
        out_shape=shape(COLS),
        input_output_aliases={0: 0},
        compiler_params=small(4),
    )(sent, rhs, before, *factors)


def advance_last(sent, before, y, high, low):
    def body(sent_ref, y_ref, before_ref, high_ref, low_ref, out_ref):
        @pl.when(lax.axis_index("row") == N_ROW - 1)
        def _():
            moved = before_ref[...]
            out_ref[...] = (y_ref[...] + mm(moved, high_ref[...]) + mm(moved, low_ref[...])).astype(BF)

    return pl.pallas_call(
        body,
        in_specs=[vmem()] * 5,
        out_specs=vmem(),
        out_shape=shape(COLS),
        input_output_aliases={0: 0},
        compiler_params=small(4),
        name="advance_last",
    )(sent, y, before, high, low)


def pack_body(blocks, tiles, count, slots, coupling_ref, out_ref, place):
    @pl.loop(0, TPR)
    def _(i):
        place[slots[0, i]] = i

    first = lax.axis_index("col") * TPD
    lane = lax.broadcasted_iota(jnp.int32, (TILE, BLK), 1)
    info = jnp.zeros((TILE, BLK), jnp.int32)
    values = []
    for k in range(KCAP):
        info = jnp.where(lane == k, blocks[k], info)
        info = jnp.where(lane == k + TILE, place[first + tiles[k]], info)
        tile = coupling_ref[k].astype(F32)
        values.append(jnp.where(k < count[0], tile, jnp.zeros_like(tile)))
        total = values[k]
        for before in range(k):
            same = (blocks[before] == blocks[k]) & (tiles[before] == tiles[k])
            total = total + jnp.where(same, values[before], jnp.zeros_like(tile))
        out_ref[k] = total.astype(BF)
    out_ref[KCAP] = info.astype(F32).astype(BF)


def pack(coupling, blocks, tiles, count, slots):
    return pl.pallas_call(
        pack_body,
        in_specs=[smem()] * 4 + [vmem()],
        out_specs=vmem(),
        out_shape=jax.ShapeDtypeStruct((KCAP + 1, TILE, BLK), BF),
        scratch_shapes=[pltpu.SMEM((TPR,), jnp.int32)],
        compiler_params=small(2),
        name="pack",
    )(blocks, tiles, count, slots, coupling)


def clear(earlier):
    def body(_, out_ref):
        out_ref[...] = jnp.zeros_like(out_ref)

    return pl.pallas_call(
        body,
        in_specs=[pl.BlockSpec(memory_space=pl.ANY)],
        out_specs=vmem(),
        out_shape=jax.ShapeDtypeStruct((N_ROW, SR, NB), BF),
        compiler_params=small(2),
        name="clear",
    )(earlier)


def build_body(cleared, c0, c1, c2, c3, out_ref, info, codes, sem):
    parts = (c0, c1, c2, c3)
    for part, ref in enumerate(parts):
        for z in range(SIDE):
            info[pl.ds(part * SIDE + z, 1)] = ref[z, KCAP].astype(F32)[:1].astype(jnp.int32)
    move = pltpu.make_async_copy(info, codes, sem)
    move.start()
    move.wait()
    for part, ref in enumerate(parts):

        @pl.loop(0, SIDE)
        def _(z):
            at = part * SIDE + z
            for k in range(KCAP):
                block = codes[at, k]
                row = pl.multiple_of(codes[at, k + TILE] * TILE, TILE)
                lane = pl.multiple_of(block % PER * BLK, BLK)
                out_ref[block // PER, pl.ds(row, TILE), pl.ds(lane, BLK)] = ref[z, k]


def build(parts, cleared):
    return pl.pallas_call(
        build_body,
        in_specs=[vmem()] * 5,
        out_specs=vmem(),
        input_output_aliases={0: 0},
        scratch_shapes=[
            pltpu.VMEM((N_COL, BLK), jnp.int32),
            pltpu.SMEM((N_COL, BLK), jnp.int32),
            pltpu.SemaphoreType.DMA(()),
        ],
        out_shape=jax.ShapeDtypeStruct((N_ROW, SR, NB), BF),
        compiler_params=small(4),
        name="build",
    )(cleared, *parts)


def group_product(c_ref, x, k, side):
    group = 2 * ((lax.axis_index("row") // 2 - k) % SIDE) + side
    return lax.dot_general(c_ref[group], x, (((1,), (1,)), ((), ())), preferred_element_type=F32)


def product_own(dense, x, k, sums=None):
    def body(c_ref, x_ref, *refs):
        part = group_product(c_ref, x_ref[...], k, lax.axis_index("row") % 2)
        refs[-1][...] = part if len(refs) == 1 else refs[0][...] + part

    more = () if sums is None else (sums,)
    return pl.pallas_call(
        body,
        in_specs=[vmem()] * (2 + len(more)),
        out_specs=vmem(),
        out_shape=jax.ShapeDtypeStruct((SR, COLS), F32),
        compiler_params=small(4),
    )(dense, x, *more)


def other_body(c_ref, x_ref, sum_ref, out_ref):
    total = sum_ref[...]
    for k in range(SIDE):
        total = total + group_product(c_ref, x_ref[k], k, 1 - lax.axis_index("row") % 2)
    out_ref[...] = total.T.astype(BF)


def products_other(dense, line, sums):
    return pl.pallas_call(
        other_body,
        in_specs=[vmem()] * 3,
        out_specs=vmem(),
        out_shape=jax.ShapeDtypeStruct((COLS, SR), BF),
        compiler_params=small(4),
        name="products_other",
    )(dense, line, sums)


def change_blocks(parts, shifts, s_ref, stacked, turned):
    col = lax.axis_index("col")
    span = SIDE * COLS
    bases = []
    for at, (ref, dx) in enumerate(zip(parts, shifts)):
        for dz in range(SIDE):
            spot = pl.multiple_of(at * span + (col % SIDE - dz) % SIDE * COLS, COLS)
            stacked[pl.ds(spot, COLS), :] = ref[dz]
        bases.append(pl.ds(pl.multiple_of((col // SIDE - dx) % SIDE * span, span), span))
    tall = SR // 3
    for n in range(s_ref.shape[1] // WIDE):
        cols = pl.ds(n * WIDE, WIDE)
        factor = jnp.concatenate([s_ref[base, cols] for base in bases], axis=0)
        if n == 0:
            for m in range(3):
                rows = pl.ds(m * tall, tall)
                turned[rows, :] = stacked[:, rows].T
                yield n, m, rows, cols, mm(turned[rows, :], factor)
        else:
            yield n, 0, pl.ds(0, SR), cols, mm(turned[...], factor)


def half_scratch():
    return [pltpu.VMEM((2 * SIDE * COLS, SR), BF), pltpu.VMEM((SR, 2 * SIDE * COLS), BF)]


def final_first(near, far, factor, schur):
    def body(w0, w1, s_ref, schur_ref, out_ref, stacked, turned):
        for _, _, rows, cols, change in change_blocks((w0, w1), (0, 1), s_ref, stacked, turned):
            out_ref[rows, cols] = schur_ref[rows, cols].astype(F32) - change

    return pl.pallas_call(
        body,
        in_specs=[vmem()] * 4,
        out_specs=vmem(),
        scratch_shapes=half_scratch(),
        out_shape=jax.ShapeDtypeStruct(schur.shape, F32),
        compiler_params=small(8),
        name="final_first",
    )(near, far, factor, schur)


def final_second(parts, factor, partial):
    def body(w2, w3, s_ref, part_ref, out_hbm, stacked, turned, out, sems):
        moves = {}
        for n, m, rows, cols, change in change_blocks((w2, w3), (2, 3), s_ref, stacked, turned):
            slot = n % SIDE
            for move in moves.pop(n - SIDE, ()):
                move.wait()
            out[slot, rows] = (part_ref[rows, cols] - change).astype(BF)
            move = pltpu.make_async_copy(out.at[slot, rows], out_hbm.at[rows, cols], sems.at[slot, m])
            move.start()
            moves.setdefault(n, []).append(move)
        for group in moves.values():
            for move in group:
                move.wait()

    return pl.pallas_call(
        body,
        in_specs=[vmem()] * 4,
        out_specs=hbm(),
        scratch_shapes=half_scratch() + [pltpu.VMEM((SIDE, SR, WIDE), BF), pltpu.SemaphoreType.DMA((SIDE, 3))],
        out_shape=jax.ShapeDtypeStruct(partial.shape, BF),
        compiler_params=small(12),
        name="final_second",
    )(*parts, factor, partial)


def turned_cols(value, dx, dz):
    pairs = [(x * SIDE + z, (x + dx) % SIDE * SIDE + (z + dz) % SIDE) for x in range(SIDE) for z in range(SIDE)]
    return lax.ppermute(value, "col", pairs)


def gather_near(value):
    return [value] + [turned_cols(value, 0, dz) for dz in (1, 2, 3)]


def gather_far(near):
    return [near] + [turned_cols(near, dx, 0) for dx in (1, 2, 3)]


def chip_shift(value, k):
    return lax.ppermute(value, "row", [(2 * a + c, 2 * ((a + k) % SIDE) + c) for a in range(SIDE) for c in (0, 1)])


def swap_cores(value):
    return lax.ppermute(value, "row", [(i, i ^ 1) for i in range(N_ROW)])


def after(value, earlier):
    return lax.optimization_barrier((value, earlier))[0]


def shards(rhs, couple_prev, diag_inverse, coupling, pair_block, pair_tile, pair_count, owner_slot, schur, surface_factor):
    sent, g_high, g_low, *upper = prep_first(rhs, couple_prev, diag_inverse)
    factors = (g_high, g_low, *upper, *prep_second(couple_prev, sent))
    near = parts = packed = cleared = last = None
    for step in range(N_ROW - 1):
        before = lax.ppermute(sent, "row", [(step, step + 1)])
        if step == 0:
            before = after(before, factors[-1])
        if step == 1:
            packed = pack(after(coupling, sent), pair_block, pair_tile, pair_count, owner_slot)
            before = after(before, packed)
        if step == 2:
            near = gather_near(packed)
        if step == 3:
            before = after(before, near)
        if step == 4:
            near = jnp.stack([near[0]] + [after(part, sent) for part in near[1:]])
            parts = gather_far(near)
            before = after(before, near)
        if step == 5:
            last = change_of(after(rhs, sent), factors)
            before = after(before, last)
        if step == 6:
            cleared = clear(sent)
            before = after(before, cleared)
        if step < N_ROW - 2:
            sent = advance(step, sent, before, rhs, factors)
        else:
            sent = advance_last(sent, before, *last)
    dense = build([parts[0]] + [after(part, sent) for part in parts[1:]], cleared)
    line = [sent] + [chip_shift(sent, k) for k in (1, 2, 3)]
    sums = product_own(dense, sent, 0)
    for k in (1, 3, 2):
        line[k] = after(line[k], sums)
        sums = product_own(dense, line[k], k, sums)
    update = products_other(dense, swap_cores(jnp.stack(line)), sums)
    pieces = [update]
    for k in (1, 2, 3):
        pieces.append(turned_cols(update, 0, k))
    near = jnp.stack(pieces)
    far = []
    for k in (1, 2, 3):
        far.append(turned_cols(near, k, 0))
    partial = final_first(near, far[0], surface_factor, schur)
    return final_second([after(part, partial) for part in far[1:]], surface_factor, partial)


def solution(mesh):
    placed = (
        P("col", "row"),
        P("row", None),
        P("row", None),
        P(("row", "col"), None, None),
        P(("row", "col")),
        P(("row", "col")),
        P(("row", "col")),
        P("row", None),
        P("row", "col"),
        P(None, "col"),
    )

    return jax.shard_map(shards, mesh=mesh, in_specs=placed, out_specs=P("row", "col"), check_vma=False)
```

```python
import jax
import jax.numpy as jnp
from jax import lax
from jax.experimental import pallas as pl
from jax.experimental.pallas import tpu as pltpu
from jax.sharding import PartitionSpec as P

NB = 1024
BLK = 128
TILE = 16
TPD = 3
KCAP = 12
TPR = 48
SR = 768
NRHS = 512
N_ROW = 8
N_COL = 16
COLS = NRHS // N_COL
PER = NB // BLK
SIDE = 4
CHUNKS = 4
WIDE = 512
EDGE = NB // 4
BF = jnp.bfloat16
F32 = jnp.float32


def split(value):
    high = value.astype(BF)
    return high, (value - high.astype(F32)).astype(BF)


def in_hbm(value):
    return pltpu.with_memory_space_constraint(value, pltpu.HBM)


def mm(left, right):
    return jnp.dot(left, right, preferred_element_type=F32)


def vmem():
    return pl.BlockSpec(memory_space=pltpu.VMEM)


def smem():
    return pl.BlockSpec(memory_space=pltpu.SMEM)


def small(limit):
    return pltpu.CompilerParams(vmem_limit_bytes=limit << 20)


def hbm():
    return pl.BlockSpec(memory_space=pltpu.HBM)


def shape(rows, kind=BF):
    return jax.ShapeDtypeStruct((rows, NB), kind)


def with_split(left, high, low):
    first, second = split(left)
    both = mm(jnp.concatenate([first, second], axis=0), high)
    return both[: left.shape[0]] + both[left.shape[0] :] + mm(first, low)


def loads(source, target, sems, first, skip):
    rows = NB // CHUNKS
    moves = []
    for at in range(target.shape[0] // rows):
        piece = source.at[pl.ds(skip + at * rows, rows)]
        moves.append(pltpu.make_async_copy(piece, target.at[pl.ds(at * rows, rows)], sems.at[first + at]))
        moves[-1].start()
    return moves


def split_arriving(moves, source, high_ref, low_ref):
    rows = NB // CHUNKS
    for at, move in enumerate(moves):
        piece = pl.ds(at * rows, rows)
        move.wait()
        high_ref[piece], low_ref[piece] = split(source[piece])


def first_body(rhs_hbm, e_hbm, g_hbm, sent_ref, g_high, g_low, e_high, e_low, rhs_in, e_in, g_in, sems):
    fetch = pltpu.make_async_copy(rhs_hbm, rhs_in, sems.at[0])
    fetch.start()
    g_moves = loads(g_hbm, g_in, sems, 1, 0)
    e_moves = loads(e_hbm, e_in, sems, 1 + CHUNKS, 0)
    fetch.wait()
    rows = NB // CHUNKS
    total = None
    for at, move in enumerate(g_moves):
        piece = pl.ds(at * rows, rows)
        move.wait()
        g_high[piece], g_low[piece] = split(g_in[piece])
        part = with_split(rhs_in[:, piece], g_high[piece], g_low[piece])
        total = part if total is None else total + part
    sent_ref[...] = total.astype(BF)
    split_arriving(e_moves, e_in, e_high, e_low)


def second_body(e_hbm, _, e_high, e_low, e_in, sems):
    split_arriving(loads(e_hbm, e_in, sems, 0, EDGE), e_in, e_high, e_low)


def prep_first(rhs, lower, inverse):
    return pl.pallas_call(
        first_body,
        in_specs=[hbm()] * 3,
        out_specs=[vmem()] * 5,
        out_shape=[shape(COLS), shape(NB), shape(NB), shape(EDGE), shape(EDGE)],
        scratch_shapes=[
            pltpu.VMEM((COLS, NB), F32),
            pltpu.VMEM((EDGE, NB), F32),
            pltpu.VMEM((NB, NB), F32),
            pltpu.SemaphoreType.DMA((1 + 2 * CHUNKS,)),
        ],
        compiler_params=small(12),
        name="prep_first",
    )(in_hbm(rhs), in_hbm(lower), in_hbm(inverse))


def prep_second(lower, earlier):
    return pl.pallas_call(
        second_body,
        in_specs=[hbm(), pl.BlockSpec(memory_space=pl.ANY)],
        out_specs=[vmem()] * 2,
        out_shape=[shape(NB - EDGE)] * 2,
        scratch_shapes=[pltpu.VMEM((NB - EDGE, NB), F32), pltpu.SemaphoreType.DMA((CHUNKS,))],
        compiler_params=small(8),
        name="prep_second",
    )(in_hbm(lower), earlier)


def change_body(rhs_ref, g_high, g_low, e0, e1, e2, e3, y_ref, high_ref, low_ref):
    rows = NB // CHUNKS

    @pl.when(lax.axis_index("row") == N_ROW - 1)
    def _():
        y_ref[...] = with_split(rhs_ref[...], g_high[...], g_low[...])
        for at in range(CHUNKS):
            high_e, low_e = (e0, e1) if at * rows < EDGE else (e2, e3)
            piece = pl.ds(at * rows - (0 if at * rows < EDGE else EDGE), rows)
            high, low = high_e[piece], low_e[piece]
            change = mm(high, g_high[...]) + mm(high, g_low[...]) + mm(low, g_high[...])
            high_ref[pl.ds(at * rows, rows)], low_ref[pl.ds(at * rows, rows)] = split(-change)


def change_of(rhs, factors):
    return pl.pallas_call(
        change_body,
        in_specs=[vmem()] * 7,
        out_specs=[vmem()] * 3,
        out_shape=[shape(COLS, F32), shape(NB), shape(NB)],
        compiler_params=small(10),
        name="change",
    )(rhs, *factors)


def advance(step, sent, before, rhs, factors):
    def body(sent_ref, rhs_ref, before_ref, g_high, g_low, e0, e1, e2, e3, out_ref):
        @pl.when(lax.axis_index("row") == step + 1)
        def _():
            upper, lower = before_ref[:, :EDGE], before_ref[:, EDGE:]
            right = rhs_ref[...] - mm(upper, e0[...]) - mm(upper, e1[...]) - mm(lower, e2[...]) - mm(lower, e3[...])
            out_ref[...] = with_split(right, g_high[...], g_low[...]).astype(BF)

    return pl.pallas_call(
        body,
        in_specs=[vmem()] * 9,
        out_specs=vmem(),
        out_shape=shape(COLS),
        input_output_aliases={0: 0},
        compiler_params=small(4),
    )(sent, rhs, before, *factors)


def advance_last(sent, before, y, high, low):
    def body(sent_ref, y_ref, before_ref, high_ref, low_ref, out_ref):
        @pl.when(lax.axis_index("row") == N_ROW - 1)
        def _():
            moved = before_ref[...]
            out_ref[...] = (y_ref[...] + mm(moved, high_ref[...]) + mm(moved, low_ref[...])).astype(BF)

    return pl.pallas_call(
        body,
        in_specs=[vmem()] * 5,
        out_specs=vmem(),
        out_shape=shape(COLS),
        input_output_aliases={0: 0},
        compiler_params=small(4),
        name="advance_last",
    )(sent, y, before, high, low)


def pack_body(blocks, tiles, count, slots, coupling_ref, out_ref, place):
    @pl.loop(0, TPR)
    def _(i):
        place[slots[0, i]] = i

    first = lax.axis_index("col") * TPD
    lane = lax.broadcasted_iota(jnp.int32, (TILE, BLK), 1)
    info = jnp.zeros((TILE, BLK), jnp.int32)
    values = []
    for k in range(KCAP):
        info = jnp.where(lane == k, blocks[k], info)
        info = jnp.where(lane == k + TILE, place[first + tiles[k]], info)
        tile = coupling_ref[k].astype(F32)
        values.append(jnp.where(k < count[0], tile, jnp.zeros_like(tile)))
        total = values[k]
        for before in range(k):
            same = (blocks[before] == blocks[k]) & (tiles[before] == tiles[k])
            total = total + jnp.where(same, values[before], jnp.zeros_like(tile))
        out_ref[k] = total.astype(BF)
    out_ref[KCAP] = info.astype(F32).astype(BF)


def pack(coupling, blocks, tiles, count, slots):
    return pl.pallas_call(
        pack_body,
        in_specs=[smem()] * 4 + [vmem()],
        out_specs=vmem(),
        out_shape=jax.ShapeDtypeStruct((KCAP + 1, TILE, BLK), BF),
        scratch_shapes=[pltpu.SMEM((TPR,), jnp.int32)],
        compiler_params=small(2),
        name="pack",
    )(blocks, tiles, count, slots, coupling)


def clear(earlier):
    def body(_, out_ref):
        out_ref[...] = jnp.zeros_like(out_ref)

    return pl.pallas_call(
        body,
        in_specs=[pl.BlockSpec(memory_space=pl.ANY)],
        out_specs=vmem(),
        out_shape=jax.ShapeDtypeStruct((N_ROW, SR, NB), BF),
        compiler_params=small(2),
        name="clear",
    )(earlier)


def build_body(cleared, c0, c1, c2, c3, out_ref, info, codes, sem):
    parts = (c0, c1, c2, c3)
    for part, ref in enumerate(parts):
        for z in range(SIDE):
            info[pl.ds(part * SIDE + z, 1)] = ref[z, KCAP].astype(F32)[:1].astype(jnp.int32)
    move = pltpu.make_async_copy(info, codes, sem)
    move.start()
    move.wait()
    for part, ref in enumerate(parts):

        @pl.loop(0, SIDE)
        def _(z):
            at = part * SIDE + z
            for k in range(KCAP):
                block = codes[at, k]
                row = pl.multiple_of(codes[at, k + TILE] * TILE, TILE)
                lane = pl.multiple_of(block % PER * BLK, BLK)
                out_ref[block // PER, pl.ds(row, TILE), pl.ds(lane, BLK)] = ref[z, k]


def build(parts, cleared):
    return pl.pallas_call(
        build_body,
        in_specs=[vmem()] * 5,
        out_specs=vmem(),
        input_output_aliases={0: 0},
        scratch_shapes=[
            pltpu.VMEM((N_COL, BLK), jnp.int32),
            pltpu.SMEM((N_COL, BLK), jnp.int32),
            pltpu.SemaphoreType.DMA(()),
        ],
        out_shape=jax.ShapeDtypeStruct((N_ROW, SR, NB), BF),
        compiler_params=small(4),
        name="build",
    )(cleared, *parts)


def group_product(c_ref, x, k, side):
    group = 2 * ((lax.axis_index("row") // 2 - k) % SIDE) + side
    return lax.dot_general(c_ref[group], x, (((1,), (1,)), ((), ())), preferred_element_type=F32)


def product_own(dense, x, k, sums=None):
    def body(c_ref, x_ref, *refs):
        part = group_product(c_ref, x_ref[...], k, lax.axis_index("row") % 2)
        refs[-1][...] = part if len(refs) == 1 else refs[0][...] + part

    more = () if sums is None else (sums,)
    return pl.pallas_call(
        body,
        in_specs=[vmem()] * (2 + len(more)),
        out_specs=vmem(),
        out_shape=jax.ShapeDtypeStruct((SR, COLS), F32),
        compiler_params=small(4),
    )(dense, x, *more)


def other_body(c_ref, x_ref, sum_ref, out_ref):
    total = sum_ref[...]
    for k in range(SIDE):
        total = total + group_product(c_ref, x_ref[k], k, 1 - lax.axis_index("row") % 2)
    out_ref[...] = total.T.astype(BF)


def products_other(dense, line, sums):
    return pl.pallas_call(
        other_body,
        in_specs=[vmem()] * 3,
        out_specs=vmem(),
        out_shape=jax.ShapeDtypeStruct((COLS, SR), BF),
        compiler_params=small(4),
        name="products_other",
    )(dense, line, sums)


def change_blocks(parts, shifts, s_ref, stacked, turned):
    col = lax.axis_index("col")
    span = SIDE * COLS
    bases = []
    for at, (ref, dx) in enumerate(zip(parts, shifts)):
        for dz in range(SIDE):
            spot = pl.multiple_of(at * span + (col % SIDE - dz) % SIDE * COLS, COLS)
            stacked[pl.ds(spot, COLS), :] = ref[dz]
        bases.append(pl.ds(pl.multiple_of((col // SIDE - dx) % SIDE * span, span), span))
    tall = SR // 3
    for n in range(s_ref.shape[1] // WIDE):
        cols = pl.ds(n * WIDE, WIDE)
        factor = jnp.concatenate([s_ref[base, cols] for base in bases], axis=0)
        if n == 0:
            for m in range(3):
                rows = pl.ds(m * tall, tall)
                turned[rows, :] = stacked[:, rows].T
                yield n, m, rows, cols, mm(turned[rows, :], factor)
        else:
            yield n, 0, pl.ds(0, SR), cols, mm(turned[...], factor)


def half_scratch():
    return [pltpu.VMEM((2 * SIDE * COLS, SR), BF), pltpu.VMEM((SR, 2 * SIDE * COLS), BF)]


def final_first(near, far, factor, schur):
    def body(w0, w1, s_ref, schur_ref, out_ref, stacked, turned):
        for _, _, rows, cols, change in change_blocks((w0, w1), (0, 1), s_ref, stacked, turned):
            out_ref[rows, cols] = schur_ref[rows, cols].astype(F32) - change

    return pl.pallas_call(
        body,
        in_specs=[vmem()] * 4,
        out_specs=vmem(),
        scratch_shapes=half_scratch(),
        out_shape=jax.ShapeDtypeStruct(schur.shape, F32),
        compiler_params=small(8),
        name="final_first",
    )(near, far, factor, schur)


def final_second(parts, factor, partial):
    def body(w2, w3, s_ref, part_ref, out_hbm, stacked, turned, out, sems):
        moves = {}
        for n, m, rows, cols, change in change_blocks((w2, w3), (2, 3), s_ref, stacked, turned):
            slot = n % SIDE
            for move in moves.pop(n - SIDE, ()):
                move.wait()
            out[slot, rows] = (part_ref[rows, cols] - change).astype(BF)
            move = pltpu.make_async_copy(out.at[slot, rows], out_hbm.at[rows, cols], sems.at[slot, m])
            move.start()
            moves.setdefault(n, []).append(move)
        for group in moves.values():
            for move in group:
                move.wait()

    return pl.pallas_call(
        body,
        in_specs=[vmem()] * 4,
        out_specs=hbm(),
        scratch_shapes=half_scratch() + [pltpu.VMEM((SIDE, SR, WIDE), BF), pltpu.SemaphoreType.DMA((SIDE, 3))],
        out_shape=jax.ShapeDtypeStruct(partial.shape, BF),
        compiler_params=small(12),
        name="final_second",
    )(*parts, factor, partial)


def turned_cols(value, dx, dz):
    pairs = [(x * SIDE + z, (x + dx) % SIDE * SIDE + (z + dz) % SIDE) for x in range(SIDE) for z in range(SIDE)]
    return lax.ppermute(value, "col", pairs)


def gather_near(value):
    return [value] + [turned_cols(value, 0, dz) for dz in (1, 2, 3)]


def gather_far(near):
    return [near] + [turned_cols(near, dx, 0) for dx in (1, 2, 3)]


def chip_shift(value, k):
    return lax.ppermute(value, "row", [(2 * a + c, 2 * ((a + k) % SIDE) + c) for a in range(SIDE) for c in (0, 1)])


def swap_cores(value):
    return lax.ppermute(value, "row", [(i, i ^ 1) for i in range(N_ROW)])


def after(value, earlier):
    return lax.optimization_barrier((value, earlier))[0]


def shards(rhs, couple_prev, diag_inverse, coupling, pair_block, pair_tile, pair_count, owner_slot, schur, surface_factor):
    sent, g_high, g_low, *upper = prep_first(rhs, couple_prev, diag_inverse)
    factors = (g_high, g_low, *upper, *prep_second(couple_prev, sent))
    near = parts = packed = cleared = last = None
    for step in range(N_ROW - 1):
        before = lax.ppermute(sent, "row", [(step, step + 1)])
        if step == 0:
            before = after(before, factors[-1])
        if step == 1:
            packed = pack(after(coupling, sent), pair_block, pair_tile, pair_count, owner_slot)
            before = after(before, packed)
        if step == 2:
            near = gather_near(packed)
        if step == 3:
            before = after(before, near)
        if step == 4:
            near = jnp.stack([near[0]] + [after(part, sent) for part in near[1:]])
            parts = gather_far(near)
            before = after(before, near)
        if step == 5:
            last = change_of(after(rhs, sent), factors)
            before = after(before, last)
        if step == 6:
            cleared = clear(sent)
            before = after(before, cleared)
        if step < N_ROW - 2:
            sent = advance(step, sent, before, rhs, factors)
        else:
            sent = advance_last(sent, before, *last)
    dense = build([parts[0]] + [after(part, sent) for part in parts[1:]], cleared)
    line = [sent]
    for k in (1, 2, 3):
        line.append(chip_shift(sent, k))
    sums = product_own(dense, sent, 0)
    for k in (1, 3, 2):
        line[k] = after(line[k], sums)
        sums = product_own(dense, line[k], k, sums)
    update = products_other(dense, swap_cores(jnp.stack(line)), sums)
    pieces = [update]
    for k in (1, 2, 3):
        pieces.append(turned_cols(update, 0, k))
    near = jnp.stack(pieces)
    far = []
    for k in (1, 2, 3):
        far.append(turned_cols(near, k, 0))
    partial = final_first(near, far[0], surface_factor, schur)
    return final_second([after(part, partial) for part in far[1:]], surface_factor, partial)


def solution(mesh):
    placed = (
        P("col", "row"),
        P("row", None),
        P("row", None),
        P(("row", "col"), None, None),
        P(("row", "col")),
        P(("row", "col")),
        P(("row", "col")),
        P("row", None),
        P("row", "col"),
        P(None, "col"),
    )

    return jax.shard_map(shards, mesh=mesh, in_specs=placed, out_specs=P("row", "col"), check_vma=False)
```
